256 devices in a mesh: seq: 16 (over y, x), pack: 16 (over z, core).
Axes of the slice: x: 4, y: 4, z: 8, core: 2. Of those that a mesh axis runs over, the one named last changes fastest.
Arguments:
- patches: bfloat16 [16, 3072, 1408], P('pack', 'seq'), may hold values from -80 to 80
- patch_mask: int32 [16, 3072], P('pack', 'seq'), may hold values 0 or 1
- mask_embed: bfloat16 [1408], replicated, may hold values from -6 to 6
- norm_gain: bfloat16 [1408], replicated, may hold values from 0.5 to 1.5
- qkv_weight: bfloat16 [1408, 4224], P(None, 'seq'), may hold values from -1 to 1
- segment_ids: int32 [16, 3072], P('pack', 'seq'), may hold values from 0 to 7, as said below
- patch_rows: int32 [16, 3072], P('pack', 'seq'), may hold values from 0 to 23, as said below
- patch_column: int32 [16, 3072], P('pack', 'seq'), may hold values from 0 to 31, as said below
- out_weight: bfloat16 [1408, 1408], replicated, may hold values from -0.625 to 0.625
- merge_gain: bfloat16 [1408], replicated, may hold values from 0.5 to 1.5
- merge_weight: bfloat16 [5632, 3584], P(None, 'seq'), may hold values from -0.078125 to 0.078125
- merge_bias: bfloat16 [3584], P('seq'), may hold values from -3 to 3
- image_owner: int32 [16, 8], P('pack'), may hold values from 0 to 15, as said below
Outputs:
- routed: bfloat16 [16, 16, 192, 3584], P('pack', None, None, 'seq')
The draws below stay inside these ranges and needn't reach their ends.
Inputs may be any that keep to these rules, and one draw needn't show every extreme that they name: `segment_ids`: in each pack the tokens come in aligned groups of four of one image (the four patches of one 2 x 2 window, in merge order); image numbers never fall along a pack; each of the 8 images has 1 to 192 groups and one has exactly 192. `patch_rows`: each image is some number w of windows wide, 1 <= w <= 16; the image with exactly 192 groups has w = 16; group g of an image covers rows 2 (g // w) and 2 (g // w) + 1 and columns 2 (g % w) and 2 (g % w) + 1, in the order (top left, top right, bottom left, bottom right). `patch_column`: as for patch_rows. `image_owner`: in each pack the owners of its 8 images are distinct owner indices, so at most 192 merged tokens go from one pack to one owner; one owner gets a pack's largest image, of exactly 192 merged tokens, from every pack.
All inputs are finite; a program needn't handle non-finite values. No bound on the sum of `patch_mask` on one device may be relied on, other than what follows from the above.
Results may differ from the reference program's by a relative error of at most 0.0061.
Values may be sent and summed in bfloat16 or wider, within the bound.
A program may use at most 64 MiB of HBM per device.

```python
import math
import jax
import jax.numpy as jnp
from jax import lax

D = 1408
HEADS = 16
HD = 88
OUT = 3584
PT = 3072
MPT = 768
PACKS = 16
IMGS = 8
MOST = 192
MERGE_IN = 5632
N_PACK = 16


def pack_layout(pack_key):
    subkeys = jax.random.split(pack_key, 4)
    weights = jax.random.randint(subkeys[0], (IMGS - 1,), 4, 9, dtype=jnp.int32)
    spare_total = MPT - MOST - (IMGS - 1)
    share_extra = spare_total * weights // jnp.sum(weights, dtype=jnp.int32)
    leftover = spare_total - jnp.sum(share_extra, dtype=jnp.int32)
    others = 1 + share_extra + (jnp.arange(IMGS - 1, dtype=jnp.int32) < leftover).astype(jnp.int32)
    largest = jax.random.randint(subkeys[1], (), 0, IMGS, dtype=jnp.int32)
    lengths = jnp.roll(jnp.concatenate([jnp.full((1,), MOST, jnp.int32), others]), largest)
    image_end = jnp.cumsum(lengths, dtype=jnp.int32)
    starts = image_end - lengths
    merged_ids = jnp.arange(MPT, dtype=jnp.int32)
    image_of = jnp.sum((merged_ids[:, None] >= image_end[None, :]).astype(jnp.int32), axis=1, dtype=jnp.int32)
    widest = min(16, MOST // 2)
    grid_rows = (MOST - 1) // widest + 1
    narrowest = jnp.clip((lengths + grid_rows - 1) // grid_rows, 1, widest)
    spread = widest - narrowest + 1
    raw = jax.random.randint(subkeys[2], (IMGS,), 0, 65536, dtype=jnp.int32)
    widths = narrowest + raw % spread
    image_index = jnp.arange(IMGS, dtype=jnp.int32)
    widths = jnp.where(image_index == largest, widest, widths)
    width_of = widths[image_of]
    offset = merged_ids - starts[image_of]
    grid_row = offset // width_of
    grid_column = offset % width_of
    quadrant = jnp.arange(4, dtype=jnp.int32)
    patch_row = (2 * grid_row[:, None] + quadrant[None, :] // 2).reshape(-1)
    patch_col = (2 * grid_column[:, None] + quadrant[None, :] % 2).reshape(-1)
    segments = jnp.repeat(image_of, 4)
    ordering = jax.random.permutation(subkeys[3], N_PACK).astype(jnp.int32)[:IMGS]
    return (segments, patch_row, patch_col, ordering, largest)


def all_layouts(key):
    layout_key = jax.random.fold_in(key, 17)
    pack_keys = jax.vmap(lambda pack_index: jax.random.fold_in(layout_key, pack_index))(jnp.arange(PACKS, dtype=jnp.int32))
    segments, patch_row, patch_col, orderings, largests = jax.vmap(pack_layout)(pack_keys)
    chosen = jax.random.randint(jax.random.fold_in(key, 29), (), 0, N_PACK, dtype=jnp.int32)

    def assign(ordering, largest):
        displaced = ordering[largest]
        swapped = jnp.where(ordering == chosen, displaced, ordering)
        return swapped.at[largest].set(chosen)
    owners = jax.vmap(assign)(orderings, largests)
    return (segments, patch_row, patch_col, owners)


def draw_segment_ids(key, part):
    return all_layouts(key)[0]


def draw_patch_rows(key, part):
    return all_layouts(key)[1]


def draw_patch_column(key, part):
    return all_layouts(key)[2]


def draw_image_owner(key, part):
    return all_layouts(key)[3]


def draw_patches(key, part):
    subkeys = jax.random.split(jax.random.fold_in(key, 53), 7)
    full_shape = (PACKS, PT, D)
    row_scale = jnp.exp(jax.random.uniform(subkeys[1], (PACKS, PT, 1), jnp.float32, math.log(0.3), math.log(3.0)))
    column_scale = jnp.exp(jax.random.uniform(subkeys[6], (D,), jnp.float32, math.log(0.3), math.log(3.0)))
    values = jax.random.normal(subkeys[0], full_shape, jnp.float32) * row_scale * column_scale
    return values.astype(jnp.bfloat16)


def draw_qkv_weight(key, part):
    subkeys = jax.random.split(jax.random.fold_in(key, 61), 1)
    weights = jax.random.normal(subkeys[0], (D, HEADS, 3, HD), jnp.float32) / math.sqrt(D)
    return weights.reshape(D, 3 * HEADS * HD).astype(jnp.bfloat16)


def plant(values, own_key, low, top_value):
    longest = values.shape.index(max(values.shape))
    spots = []
    for shift in (0, 1):
        where = [jax.random.randint(jax.random.fold_in(own_key, axis), (), 0, length) for axis, length in enumerate(values.shape)]
        where[longest] = (where[longest] + shift) % values.shape[longest]
        spots.append(tuple(where))
    return values.at[spots[0]].set(low).at[spots[1]].set(top_value)


def steps_of(stream_key, dims, shards, low, high):
    gain, own = 1.0, jax.random.fold_in(stream_key, 6)
    for position, blocks in shards:
        steps = jnp.exp(jax.random.uniform(jax.random.fold_in(own, position), (blocks,), jnp.float32, low / len(shards), high / len(shards)))
        gain = gain * jnp.repeat(steps, dims[position] // blocks).reshape([-1 if axis == position else 1 for axis in range(len(dims))])
    return gain


def normal_values(key, shape, scale, most, shards=(), kind=jnp.bfloat16):
    drawn = jax.random.normal(key, shape, jnp.float32) * scale
    if len(shards) > 0:
        drawn = steps_of(key, shape, shards, -0.22, 0.18) * drawn
    return jnp.clip(drawn, min=-most, max=most).astype(kind)


def setup_inputs(seed: int = 0) -> dict:
    seeds = jax.random.split(jax.random.key(seed), 14)
    return {
        "patches": draw_patches(jax.random.fold_in(seeds[13], 71), 0),
        "patch_mask": plant((jax.random.randint(seeds[1], (PACKS, PT), 0, 4) < 1).astype(jnp.int32), jax.random.fold_in(seeds[1], 1), 0, 1),
        "mask_embed": normal_values(seeds[2], (D,), 1.0, 6.0),
        "norm_gain": jnp.clip(jax.random.uniform(seeds[3], (D,), jnp.float32, 0.5, 1.5), 0.5, 1.5).astype(jnp.bfloat16),
        "qkv_weight": draw_qkv_weight(jax.random.fold_in(seeds[13], 71), 0),
        "segment_ids": draw_segment_ids(jax.random.fold_in(seeds[13], 71), 0),
        "patch_rows": draw_patch_rows(jax.random.fold_in(seeds[13], 71), 0),
        "patch_column": draw_patch_column(jax.random.fold_in(seeds[13], 71), 0),
        "out_weight": normal_values(seeds[8], (D, D), HD ** -0.5, 0.625),
        "merge_gain": jnp.clip(jax.random.uniform(seeds[9], (D,), jnp.float32, 0.5, 1.5), 0.5, 1.5).astype(jnp.bfloat16),
        "merge_weight": normal_values(seeds[10], (MERGE_IN, OUT), MERGE_IN ** -0.5, 0.078125, ((1, 16),)),
        "merge_bias": normal_values(seeds[11], (OUT,), 0.5, 3.0, ((0, 16),)),
        "image_owner": draw_image_owner(jax.random.fold_in(seeds[13], 71), 0),
    }


EPSILON = 1e-06

def layer_norm(values, gain_vector):
    center = values - lax.optimization_barrier(jnp.mean(values, axis=-1, keepdims=True))
    spread = lax.optimization_barrier(jnp.mean(center * center, axis=-1, keepdims=True))
    return center * lax.rsqrt(spread + EPSILON) * gain_vector.astype(jnp.float32)

def rotate(vectors, row_index, column_index):
    total_rows, heads_here, head_width = vectors.shape
    quarter = head_width // 4
    frequency = 10000.0 ** (-jnp.arange(quarter, dtype=jnp.float32) / quarter)
    row_angle = row_index.astype(jnp.float32)[:, None] * frequency[None, :]
    column_angle = column_index.astype(jnp.float32)[:, None] * frequency[None, :]
    angles = jnp.stack([row_angle, column_angle], axis=1)[:, None, :, None, :]
    split_up = vectors.reshape(total_rows, heads_here, 2, 2, quarter)
    partner = jnp.stack([-split_up[:, :, :, 1], split_up[:, :, :, 0]], axis=3)
    turned = split_up * jnp.cos(angles) + partner * jnp.sin(angles)
    return turned.reshape(total_rows, heads_here, head_width)

def qkv_block(projected, row_index, column_index):
    turned_queries = rotate(projected[:, :, 0], row_index, column_index)
    turned_keys = rotate(projected[:, :, 1], row_index, column_index)
    return jnp.concatenate([turned_queries, turned_keys, projected[:, :, 2]], axis=-1).astype(jnp.bfloat16)

def attention(block, segments):
    total_rows, heads_here, triple = block.shape
    head_width = triple // 3
    step_rows = min(512, total_rows)
    query_part = block[:, :, :head_width].reshape(total_rows // step_rows, step_rows, heads_here, head_width)
    key_part = block[:, :, head_width:2 * head_width].astype(jnp.float32)
    value_part = block[:, :, 2 * head_width:].astype(jnp.float32)
    query_segments = segments.reshape(total_rows // step_rows, step_rows)
    scale = head_width ** (-0.5)

    def one_block(inputs_pair):
        queries_here, segments_here = inputs_pair
        scores = jnp.einsum('qhd,khd->hqk', queries_here.astype(jnp.float32), key_part) * scale
        same_image = (segments_here[:, None] == segments[None, :])[None]
        scores = jnp.where(same_image, scores, -jnp.inf)
        highest = lax.optimization_barrier(jnp.max(scores, axis=-1, keepdims=True))
        weights = jnp.exp(scores - highest)
        probs = (weights / lax.optimization_barrier(jnp.sum(weights, axis=-1, keepdims=True))).astype(jnp.bfloat16)
        result = jnp.einsum('hqk,khd->qhd', probs.astype(jnp.float32), value_part)
        return result.astype(jnp.bfloat16)
    return lax.map(one_block, (query_part, query_segments)).reshape(total_rows, heads_here, head_width)

def route(projected, segments, owners_here, packs, most):
    merged_segments = segments[::4]
    images = owners_here.shape[0]
    image_ids = jnp.arange(images, dtype=jnp.int32)
    member = (merged_segments[None, :] == image_ids[:, None]).astype(jnp.int32)
    lengths = lax.optimization_barrier(jnp.sum(member, axis=1, dtype=jnp.int32))
    starts = jnp.cumsum(lengths, dtype=jnp.int32) - lengths
    owner_ids = jnp.arange(packs, dtype=jnp.int32)
    owned = owners_here[None, :] == owner_ids[:, None]
    first_row = lax.optimization_barrier(jnp.sum(jnp.where(owned, starts[None, :], 0), axis=1, dtype=jnp.int32))
    owned_length = lax.optimization_barrier(jnp.sum(jnp.where(owned, lengths[None, :], 0), axis=1, dtype=jnp.int32))
    slots = jnp.arange(most, dtype=jnp.int32)
    source_rows = jnp.clip(first_row[:, None] + slots[None, :], 0, projected.shape[0] - 1)
    picked = jnp.take(projected, source_rows.reshape(-1), axis=0).reshape(packs, most, projected.shape[1])
    filled = slots[None, :] < owned_length[:, None]
    return jnp.where(filled[:, :, None], picked, jnp.zeros_like(picked))

def reference(patches, patch_mask, mask_embed, norm_gain, qkv_weight, segment_ids, patch_rows, patch_column, out_weight, merge_gain, merge_weight, merge_bias, image_owner):

    def encode_pack(pack_inputs):
        patches_here, mask_here, segments, row_index, column_index, owners_here = pack_inputs
        inputs = jnp.where(mask_here[:, None] == 1, mask_embed[None, :], patches_here)
        normed = layer_norm(inputs.astype(jnp.float32), norm_gain).astype(jnp.bfloat16)
        projected = jnp.dot(normed, qkv_weight, preferred_element_type=jnp.float32)
        block = qkv_block(projected.reshape(PT, HEADS, 3, HD), row_index, column_index)
        attended = attention(block, segments).reshape(PT, D)
        residual = inputs.astype(jnp.float32) + jnp.dot(attended, out_weight, preferred_element_type=jnp.float32)
        merged = layer_norm(residual, merge_gain).astype(jnp.bfloat16).reshape(MPT, MERGE_IN)
        projected_merged = (jnp.dot(merged, merge_weight, preferred_element_type=jnp.float32) + merge_bias.astype(jnp.float32)).astype(jnp.bfloat16)
        return route(projected_merged, segments, owners_here, N_PACK, MOST)
    routed = lax.map(encode_pack, (patches, patch_mask, segment_ids, patch_rows, patch_column, image_owner))
    return jnp.swapaxes(routed, 0, 1)
```

```python
import functools

import jax
import jax.numpy as jnp
from jax import lax
from jax.experimental import pallas as pl
from jax.experimental.pallas import tpu as pltpu
from jax.sharding import PartitionSpec as P

D = 1408
HEADS = 16
HD = 88
ROWS = 192
GROUPS = 48
OUTC = 224
MOST = 192
EPSILON = 1e-06
F32 = jnp.float32
BF16 = jnp.bfloat16
MESH = pl.DeviceIdType.MESH
NT = (((1,), (1,)), ((), ()))
VM = pl.BlockSpec(memory_space=pltpu.VMEM)
SM = pl.BlockSpec(memory_space=pltpu.SMEM)


def iota(shape, axis):
    return lax.broadcasted_iota(jnp.int32, shape, axis)


def column_of(row):
    n = row.shape[1]
    eye = (iota((n, n), 0) == iota((n, n), 1)).astype(BF16)
    wide = jnp.broadcast_to(row, (8, n)).astype(BF16)
    return lax.dot_general(eye, wide, NT, preferred_element_type=F32)[:, :1]


def side_by_side(left, right):
    n = left.shape[1]
    first = (iota((n, 2 * n), 0) == iota((n, 2 * n), 1)).astype(BF16)
    second = (iota((n, 2 * n), 0) + n == iota((n, 2 * n), 1)).astype(BF16)
    return jnp.dot(left.astype(BF16), first, preferred_element_type=F32) + jnp.dot(
        right.astype(BF16), second, preferred_element_type=F32
    )


def layer_norm(values, gain):
    center = values - jnp.mean(values, axis=-1, keepdims=True)
    spread = jnp.mean(center * center, axis=-1, keepdims=True)
    return center * lax.rsqrt(spread + EPSILON) * gain


def embedded(patches_ref, mask_ref, embed_ref):
    chosen = column_of(mask_ref[...].astype(F32))
    return jnp.where(
        chosen > 0.5, embed_ref[...].astype(F32), patches_ref[0].astype(F32)
    )


def qkv_kernel(
    patches_ref,
    mask_ref,
    embed_ref,
    gain_ref,
    weight_ref,
    seg_ref,
    row_ref,
    col_ref,
    out_ref,
    labels_ref,
    tok,
    wts,
    prod,
    relay,
    mine,
    t_send,
    t_recv,
    w_send,
    w_recv,
    p_send,
    p_recv,
    m_send,
    m_recv,
):
    s = lax.axis_index("seq")
    core = lax.rem(lax.axis_index("pack"), 2)
    y, x = s // 4, lax.rem(s, 4)
    a = x * (1 - core) + y * core
    b = y * (1 - core) + x * core
    step_a, step_b = 1 + 3 * core, 4 - 3 * core

    def on_a(k):
        return {"seq": lax.rem(a + k, 4) * step_a + b * step_b}

    def on_b(k):
        return {"seq": a * step_a + lax.rem(b + k, 4) * step_b}

    barrier = pltpu.get_barrier_semaphore()
    for d in range(1, 16):
        pl.semaphore_signal(
            barrier, inc=1, device_id={"seq": lax.rem(s + d, 16)}, device_id_type=MESH
        )

    mine[0:1, :] = seg_ref[...]
    mine[1:2, :] = row_ref[...]
    mine[2:3, :] = col_ref[...]
    mine[3:8, :] = jnp.zeros((5, ROWS), jnp.int32)
    labels_ref[s] = mine[...]
    inputs = embedded(patches_ref, mask_ref, embed_ref)
    tok[a] = layer_norm(inputs, gain_ref[...].astype(F32)).astype(BF16)
    wts[b] = weight_ref[...]
    pl.semaphore_wait(barrier, 15)

    def copy(src, dst, send, recv, k, where):
        return pltpu.make_async_remote_copy(
            src_ref=src,
            dst_ref=dst,
            send_sem=send.at[k],
            recv_sem=recv.at[k],
            device_id=where,
            device_id_type=MESH,
        )

    def ring(buf, pos, cut, size, send, recv, to):
        upper, lower = pl.ds(0, cut), pl.ds(cut, size - cut)
        before, after = lax.rem(pos + 3, 4), lax.rem(pos + 1, 4)

        def one(slot, part, k, where):
            ref = buf.at[slot, part]
            return copy(ref, ref, send, recv, k, where)

        return [
            one(pos, upper, 0, to(1)),
            one(pos, lower, 1, to(3)),
            one(pos, lower, 2, to(1)),
            one(pos, upper, 3, to(3)),
            one(before, upper, 4, to(1)),
            one(after, lower, 5, to(3)),
        ]

    w_ring = ring(wts, b, 136, 264, w_send, w_recv, on_b)
    t_ring = ring(tok, a, 96, ROWS, t_send, t_recv, on_a)
    for k in range(4):
        w_ring[k].start()
        t_ring[k].start()
    labels = []
    for d in range(1, 16):
        labels.append(
            copy(mine, labels_ref.at[s], m_send, m_recv, d, {"seq": lax.rem(s + d, 16)})
        )
        labels[-1].start()
    for one in labels:
        one.wait_recv()

    feature = iota((HD, 1), 0)
    quarter = HD // 4
    place = lax.rem(feature, quarter).astype(F32)
    frequency = jnp.exp(place * (-9.210340371976184 / quarter))
    is_row = feature < 2 * quarter
    is_first = lax.rem(feature, 2 * quarter) < quarter

    def table(pair):
        left = labels_ref[(2 * pair) * step_a + b * step_b].astype(F32)
        right = labels_ref[(2 * pair + 1) * step_a + b * step_b].astype(F32)
        both = side_by_side(left, right)
        angle = jnp.where(is_row, both[1:2], both[2:3]) * frequency
        sine = jnp.sin(angle)
        return jnp.cos(angle), jnp.where(is_first, -sine, 0.0), jnp.where(is_first, 0.0, sine)

    pairs = (a // 2, 1 - a // 2)
    tables = [table(pair) for pair in pairs]

    t_ring[0].wait_recv()
    t_ring[4].start()
    t_ring[1].wait_recv()
    t_ring[5].start()
    w_ring[0].wait_recv()
    w_ring[4].start()
    w_ring[1].wait_recv()
    w_ring[5].start()
    t_ring[2].wait_recv()
    t_ring[3].wait_recv()
    w_ring[2].wait_recv()
    w_ring[3].wait_recv()

    def turn(part, k):
        cosine, ahead, behind = tables[k]
        return (
            part * cosine
            + pltpu.roll(part, HD - quarter, 0) * ahead
            + pltpu.roll(part, quarter, 0) * behind
        )

    def block(k, head):
        tokens = tok[pl.ds(2 * pairs[k], 2)].reshape(2 * ROWS, D)
        projected = lax.dot_general(wts[head], tokens, NT, preferred_element_type=F32)
        return jnp.concatenate(
            [turn(projected[:HD], k), turn(projected[HD : 2 * HD], k), projected[2 * HD :]],
            axis=0,
        ).astype(BF16)

    up, down, far = lax.rem(b + 1, 4), lax.rem(b + 3, 4), lax.rem(b + 2, 4)
    sends = {}

    def send_to(k, head, n, where, slot):
        prod[slot] = block(k, head)
        sends[n] = copy(prod.at[slot], out_ref.at[b, pairs[k]], p_send, p_recv, n, where)
        sends[n].start()

    def send_far(k, n, where, slot):
        prod[slot] = block(k, far)
        sends[n] = copy(prod.at[slot], relay.at[k], p_send, p_recv, n, where)
        sends[n].start()

    send_to(0, up, 0, on_b(1), 0)
    send_to(0, down, 2, on_b(3), 1)
    w_ring[4].wait_recv()
    w_ring[5].wait_recv()
    send_far(0, 4, on_b(1), 2)
    t_ring[4].wait_recv()
    t_ring[5].wait_recv()
    send_far(1, 5, on_b(3), 3)
    send_to(1, up, 1, on_b(1), 4)
    send_to(1, down, 3, on_b(3), 5)
    out_ref[b, pairs[0]] = block(0, b)
    sends[4].wait_recv()
    sends[6] = copy(relay.at[0], out_ref.at[down, pairs[0]], p_send, p_recv, 6, on_b(1))
    sends[6].start()
    sends[5].wait_recv()
    sends[7] = copy(relay.at[1], out_ref.at[up, pairs[1]], p_send, p_recv, 7, on_b(3))
    sends[7].start()
    out_ref[b, pairs[1]] = block(1, b)
    for n in (0, 1, 2, 3, 6, 7):
        sends[n].wait_recv()
    for one in w_ring + t_ring + labels + list(sends.values()):
        one.wait_send()


def attention_kernel(n_pack, qkv_ref, labels_ref, owner_ref, out_ref, table_ref, qs, kvs, segs):
    core = lax.rem(lax.axis_index("pack"), 2)
    half = ROWS
    wide = 2 * ROWS

    @pl.when(core == 0)
    def _():
        for m in range(8):
            kvs[m] = qkv_ref[m // 2, m % 2]

    @pl.when(core == 1)
    def _():
        lane = iota((3 * HD, wide), 1)
        for m in range(8):
            second, j = (m // 2) % 2, m // 4
            left = qkv_ref[2 * (m % 2), j].astype(F32)
            right = qkv_ref[2 * (m % 2) + 1, j].astype(F32)
            if second:
                left = pltpu.roll(left, half, 1)
            else:
                right = pltpu.roll(right, half, 1)
            kvs[m] = jnp.where(lane < half, left, right).astype(BF16)

    for m in range(8):
        turned = jnp.concatenate(
            [kvs[m].astype(F32)[:HD], jnp.zeros((128 - HD, wide), F32)], axis=0
        ).T
        qs[2 * m] = turned[:half].astype(BF16)
        qs[2 * m + 1] = turned[half:].astype(BF16)
        segs[m] = side_by_side(
            labels_ref[2 * m].astype(F32), labels_ref[2 * m + 1].astype(F32)
        )

    every = jnp.concatenate([labels_ref[k][0:1] for k in range(16)], axis=0)
    total = 16 * ROWS
    starts = [jnp.int32(0)]
    for image in range(1, 8):
        starts.append(jnp.sum((every < image).astype(jnp.int32)))
    starts.append(jnp.int32(total))
    lane = iota((1, 128), 1)
    first = jnp.zeros((1, 128), jnp.int32)
    length = jnp.zeros((1, 128), jnp.int32)
    for image in range(8):
        mine = lane == owner_ref[0, image]
        first = jnp.where(mine, starts[image] // 4, first)
        length = jnp.where(mine, (starts[image + 1] - starts[image]) // 4, length)
    table_ref[0:1, :] = first
    table_ref[1:2, :] = length
    table_ref[2:8, :] = jnp.zeros((6, 128), jnp.int32)

    scale = HD ** (-0.5) * 1.4426950408889634
    low = -0.7 * 3.4028235e38

    def one_block(s, carry):
        begin = jnp.int32(0)
        end = jnp.int32(total)
        for image in range(1, 8):
            begin = jnp.where(starts[image] <= s * ROWS, starts[image], begin)
        for image in range(7, 0, -1):
            end = jnp.where(starts[image] >= (s + 1) * ROWS, starts[image], end)
        queries = qs[s][:, :HD]
        own = column_of(labels_ref[s][0:1].astype(F32))

        def one_step(m, state):
            top, denominator, acc = state
            scores = jnp.dot(queries, kvs[m, pl.ds(HD, HD)], preferred_element_type=F32)
            scores = jnp.where(own == segs[m][0:1], scores, low)
            new_top = jnp.maximum(top, jnp.max(scores, axis=-1, keepdims=True))
            shrink = jnp.exp2((top - new_top) * scale)
            weights = jnp.exp2((scores - new_top) * scale)
            denominator = denominator * shrink + jnp.sum(weights, axis=-1, keepdims=True)
            acc = acc * shrink + lax.dot_general(
                weights.astype(BF16), kvs[m, pl.ds(2 * HD, HD)], NT, preferred_element_type=F32
            )
            return new_top, denominator, acc

        state = (
            jnp.full((ROWS, 1), low, F32),
            jnp.zeros((ROWS, 1), F32),
            jnp.zeros((ROWS, HD), F32),
        )
        _, denominator, acc = lax.fori_loop(
            begin // wide, (end + wide - 1) // wide, one_step, state
        )
        out_ref[s] = (acc / denominator).astype(BF16)
        return carry

    lax.fori_loop(0, 16, one_block, 0)


def merge_kernel(
    n_pack,
    att_ref,
    patches_ref,
    mask_ref,
    embed_ref,
    wo_ref,
    gain_ref,
    wm_ref,
    bias_ref,
    table_ref,
    rows_ref,
    tables_ref,
    heads,
    acc,
    tiles,
    mg,
    h_send,
    h_recv,
    g_send,
    g_recv,
    z_send,
    z_recv,
    c_send,
    c_recv,
    b_send,
    b_recv,
):
    s = lax.axis_index("seq")
    p = lax.axis_index("pack")
    nz = n_pack // 2
    z, core = p // 2, lax.rem(p, 2)
    y, x = s // 4, lax.rem(s, 4)

    barrier = pltpu.get_barrier_semaphore()
    for d in range(1, 16):
        pl.semaphore_signal(
            barrier, inc=1, device_id={"seq": lax.rem(s + d, 16)}, device_id_type=MESH
        )
    for d in range(1, n_pack):
        pl.semaphore_signal(
            barrier, inc=1, device_id={"pack": lax.rem(p + d, n_pack)}, device_id_type=MESH
        )
    pl.semaphore_wait(barrier, 15 + n_pack - 1)

    def copy(src, dst, send, recv, k, where):
        return pltpu.make_async_remote_copy(
            src_ref=src,
            dst_ref=dst,
            send_sem=send.at[k],
            recv_sem=recv.at[k],
            device_id=where,
            device_id_type=MESH,
        )

    out = []
    back = []
    for d in range(1, 16):
        to = lax.rem(s + d, 16)
        back.append(copy(att_ref.at[to], heads.at[s], h_send, h_recv, d, {"seq": to}))
        back[-1].start()
    tabs = []
    for d in range(1, n_pack):
        tabs.append(
            copy(table_ref, tables_ref.at[p], b_send, b_recv, d, {"pack": lax.rem(p + d, n_pack)})
        )
        tabs[-1].start()
    tables_ref[p] = table_ref[...]
    out += back + tabs
    inputs = embedded(patches_ref, mask_ref, embed_ref)
    acc[...] = inputs + jnp.dot(att_ref[s], wo_ref[s], preferred_element_type=F32)
    for d in range(1, 16):
        back[d - 1].wait_recv()
        head = lax.rem(s + 16 - d, 16)
        acc[...] += jnp.dot(heads[head], wo_ref[head], preferred_element_type=F32)
    normed = layer_norm(acc[...], gain_ref[...].astype(F32))
    for t in range(D // 128):
        tiles[t] = normed[:, 128 * t : 128 * (t + 1)]
    for t in range(D // 128):
        for j in range(4):
            mg[s, j, :, 128 * t : 128 * (t + 1)] = tiles[t, pl.ds(j, GROUPS, stride=4), :].astype(
                BF16
            )

    order = {0: 0, -1: 1, 1: 2, 2: 3}

    def device(half, df, dg):
        dx, dy = (df, dg) if half == 0 else (dg, df)
        return lax.rem(y + dy + 4, 4) * 4 + lax.rem(x + dx + 4, 4)

    started = {}

    def send(half, phase, df, dg, kind):
        k = ((half * 2 + phase) * 4 + (order[df] if phase else 0)) * 4 + kind
        blk = device(half, df, dg)
        step = 1 if kind in (0, 2) else -1
        to = device(half, 0, step) if phase else device(half, step, 0)
        if kind < 2:
            ref = mg.at[blk, pl.ds(2 * half, 2)]
        else:
            ref = mg.at[blk, pl.ds(2 * half + kind - 2, 1)]
        one = copy(ref, ref, g_send, g_recv, k, {"seq": to})
        one.start()
        started[half, phase, order[df] if phase else 0, kind] = one
        out.append(one)

    def arrive(half, df, dg):
        phase = 0 if dg == 0 else 1
        off = df if phase == 0 else dg
        k = order[df] if phase else 0
        if off == 2:
            started[half, phase, k, 2].wait_recv()
            started[half, phase, k, 3].wait_recv()
        elif off == -1:
            started[half, phase, k, 0].wait_recv()
            send(half, phase, df, dg, 2)
        else:
            started[half, phase, k, 1].wait_recv()
            send(half, phase, df, dg, 3)
        if phase == 0:
            send(half, 1, df, 0, 0)
            send(half, 1, df, 0, 1)

    done = set()

    def need(half, df, dg):
        if (half, df, dg) not in done and (df, dg) != (0, 0):
            done.add((half, df, dg))
            arrive(half, df, dg)

    z_out = {}

    def z_copy(ref, k, step, c):
        if step == 2:
            return copy(ref, ref, c_send, c_recv, c * nz + k, {"pack": z * 2 + 1 - core})
        to = lax.rem(z + step + nz, nz) * 2 + core
        return copy(ref, ref, z_send, z_recv, (c * 2 + (step + 1) // 2) * nz + k, {"pack": to})

    def chunk(c, dy):
        row = lax.rem(y + dy + 4, 4)
        total = jnp.broadcast_to(bias_ref[...].astype(F32), (4 * GROUPS, OUTC))
        for j in range(4):
            part = mg[pl.ds(4 * row, 4), j].reshape(4 * GROUPS, D)
            total += lax.dot_general(
                part, wm_ref[:, pl.ds(j * D, D)], NT, preferred_element_type=F32
            )
        rows_ref[p, row] = total.astype(BF16)
        own = rows_ref.at[p, row]
        for step in (1, -1, 2):
            z_out[c, step, 0] = z_copy(own, 0, step, c)
            z_out[c, step, 0].start()

    def hops(c):
        return (nz // 2, nz - 1 - nz // 2) if c % 2 == 0 else (nz - 1 - nz // 2, nz // 2)

    def pass_on(c, dy):
        row = lax.rem(y + dy + 4, 4)
        limits = hops(c)
        for h in range(1, max(limits) + 1):
            for step, limit in ((1, limits[0]), (-1, limits[1])):
                if h > limit:
                    continue
                z_out[c, step, h - 1].wait_recv()
                pack = lax.rem(z - step * h + nz, nz) * 2 + core
                ref = rows_ref.at[pack, row]
                if h < limit:
                    z_out[c, step, h] = z_copy(ref, h, step, c)
                    z_out[c, step, h].start()
                k = h if step == 1 else limits[0] + h
                z_out[c, 2, k] = z_copy(ref, k, 2, c)
                z_out[c, 2, k].start()

    for half in range(2):
        send(half, 0, 0, 0, 0)
        send(half, 0, 0, 0, 1)
    for half in range(2):
        send(half, 1, 0, 0, 0)
        send(half, 1, 0, 0, 1)
    for half in range(2):
        need(half, -1, 0)
        need(half, 1, 0)
    for half in range(2):
        need(half, 0, -1)
        need(half, 0, 1)
    for half in range(2):
        need(half, 2, 0)

    def row_ready(dy):
        for dx in (0, -1, 1, 2):
            need(0, dx, dy)
            need(1, dy, dx)

    row_ready(0)
    chunk(0, 0)
    for df in (-1, 1, 2):
        for dg in (-1, 1):
            for half in range(2):
                need(half, df, dg)
    row_ready(-1)
    chunk(1, -1)
    pass_on(0, 0)
    row_ready(1)
    chunk(2, 1)
    pass_on(1, -1)
    row_ready(2)
    chunk(3, 2)
    pass_on(2, 1)
    pass_on(3, 2)
    for c in range(4):
        for k in range(nz):
            z_out[c, 2, k].wait_recv()
    for one in tabs:
        one.wait_recv()
    for one in out + list(z_out.values()):
        one.wait_send()


def select_kernel(n_pack, rows_ref, tables_ref, out_ref):
    p = lax.axis_index("pack")
    total = 4 * MOST
    window = MOST + 16
    for q in range(n_pack):
        mine = iota((1, 128), 1) == p
        first = jnp.sum(jnp.where(mine, tables_ref[q, 0:1, :], 0))
        length = jnp.sum(jnp.where(mine, tables_ref[q, 1:2, :], 0))
        base = pl.multiple_of(jnp.minimum((first // 16) * 16, total - window), 16)
        slot = iota((MOST, window), 0)
        source = iota((MOST, window), 1)
        pick = ((source == slot + (first - base)) & (slot < length)).astype(BF16)
        out_ref[0, q] = jnp.dot(
            pick, rows_ref[q, pl.ds(base, window)], preferred_element_type=F32
        ).astype(BF16)


def local(
    patches,
    patch_mask,
    mask_embed,
    norm_gain,
    qkv_weight,
    segment_ids,
    patch_rows,
    patch_column,
    out_weight,
    merge_gain,
    merge_weight,
    merge_bias,
    image_owner,
):
    n_pack = lax.axis_size("pack")
    nz = n_pack // 2
    dma = pltpu.SemaphoreType.DMA
    shape = jax.ShapeDtypeStruct
    embed = mask_embed[None, :]
    qkv, labels = pl.pallas_call(
        qkv_kernel,
        out_shape=(shape((4, 2, 3 * HD, 2 * ROWS), BF16), shape((16, 8, ROWS), jnp.int32)),
        in_specs=[VM] * 8,
        out_specs=(VM, VM),
        scratch_shapes=[
            pltpu.VMEM((4, ROWS, D), BF16),
            pltpu.VMEM((4, 3 * HD, D), BF16),
            pltpu.VMEM((6, 3 * HD, 2 * ROWS), BF16),
            pltpu.VMEM((2, 3 * HD, 2 * ROWS), BF16),
            pltpu.VMEM((8, ROWS), jnp.int32),
            dma((6,)),
            dma((6,)),
            dma((6,)),
            dma((6,)),
            dma((8,)),
            dma((8,)),
            dma((16,)),
            dma((16,)),
        ],
        compiler_params=pltpu.CompilerParams(
            collective_id=0, has_side_effects=True, vmem_limit_bytes=60 * 2**20
        ),
        name="qkv",
    )(
        patches,
        patch_mask,
        embed,
        norm_gain[None, :],
        qkv_weight.T,
        segment_ids,
        patch_rows,
        patch_column,
    )
    attended, table = pl.pallas_call(
        functools.partial(attention_kernel, n_pack),
        out_shape=(shape((16, ROWS, HD), BF16), shape((8, 128), jnp.int32)),
        in_specs=[VM, VM, SM],
        out_specs=(VM, VM),
        scratch_shapes=[
            pltpu.VMEM((16, ROWS, 128), BF16),
            pltpu.VMEM((8, 3 * HD, 2 * ROWS), BF16),
            pltpu.VMEM((8, 8, 2 * ROWS), F32),
        ],
        compiler_params=pltpu.CompilerParams(vmem_limit_bytes=60 * 2**20),
        name="attention",
    )(qkv, labels, image_owner)
    rows, tables = pl.pallas_call(
        functools.partial(merge_kernel, n_pack),
        out_shape=(
            shape((n_pack, 4, 4 * GROUPS, OUTC), BF16),
            shape((n_pack, 8, 128), jnp.int32),
        ),
        in_specs=[VM] * 9,
        out_specs=(VM, VM),
        scratch_shapes=[
            pltpu.VMEM((16, ROWS, HD), BF16),
            pltpu.VMEM((ROWS, D), F32),
            pltpu.VMEM((D // 128, ROWS, 128), F32),
            pltpu.VMEM((16, 4, GROUPS, D), BF16),
            dma((16,)),
            dma((16,)),
            dma((64,)),
            dma((64,)),
            dma((8 * nz,)),
            dma((8 * nz,)),
            dma((4 * nz,)),
            dma((4 * nz,)),
            dma((n_pack,)),
            dma((n_pack,)),
        ],
        compiler_params=pltpu.CompilerParams(
            collective_id=1, has_side_effects=True, vmem_limit_bytes=60 * 2**20
        ),
        name="merge",
    )(
        attended,
        patches,
        patch_mask,
        embed,
        out_weight.reshape(HEADS, HD, D),
        merge_gain[None, :],
        merge_weight.T,
        merge_bias[None, :],
        table,
    )
    return pl.pallas_call(
        functools.partial(select_kernel, n_pack),
        out_shape=shape((1, n_pack, MOST, OUTC), BF16),
        in_specs=[VM, VM],
        out_specs=VM,
        compiler_params=pltpu.CompilerParams(vmem_limit_bytes=60 * 2**20),
        name="select",
    )(rows.reshape(n_pack, 4 * MOST, OUTC), tables)


def solution(mesh):
    placed = (
        P("pack", "seq", None),
        P("pack", "seq"),
        P(),
        P(),
        P(None, "seq"),
        P("pack", "seq"),
        P("pack", "seq"),
        P("pack", "seq"),
        P(),
        P(),
        P(None, "seq"),
        P("seq"),
        P("pack", None),
    )
    return jax.shard_map(
        local, mesh=mesh, in_specs=placed, out_specs=P("pack", None, None, "seq"), check_vma=False
    )
```

```python
import functools

import jax
import jax.numpy as jnp
from jax import lax
from jax.experimental import pallas as pl
from jax.experimental.pallas import tpu as pltpu
from jax.sharding import PartitionSpec as P

D = 1408
HEADS = 16
HD = 88
ROWS = 192
GROUPS = 48
OUTC = 224
MOST = 192
EPSILON = 1e-06
F32 = jnp.float32
BF16 = jnp.bfloat16
MESH = pl.DeviceIdType.MESH
NT = (((1,), (1,)), ((), ()))
VM = pl.BlockSpec(memory_space=pltpu.VMEM)
ANY = pl.BlockSpec(memory_space=pl.ANY)
SM = pl.BlockSpec(memory_space=pltpu.SMEM)


def iota(shape, axis):
    return lax.broadcasted_iota(jnp.int32, shape, axis)


def column_of(row):
    n = row.shape[1]
    eye = (iota((n, n), 0) == iota((n, n), 1)).astype(BF16)
    wide = jnp.broadcast_to(row, (8, n)).astype(BF16)
    return lax.dot_general(eye, wide, NT, preferred_element_type=F32)[:, :1]


def side_by_side(left, right):
    n = left.shape[1]
    first = (iota((n, 2 * n), 0) == iota((n, 2 * n), 1)).astype(BF16)
    second = (iota((n, 2 * n), 0) + n == iota((n, 2 * n), 1)).astype(BF16)
    return jnp.dot(left.astype(BF16), first, preferred_element_type=F32) + jnp.dot(
        right.astype(BF16), second, preferred_element_type=F32
    )


def layer_norm(values, gain):
    center = values - jnp.mean(values, axis=-1, keepdims=True)
    spread = jnp.mean(center * center, axis=-1, keepdims=True)
    return center * lax.rsqrt(spread + EPSILON) * gain


def embedded(patches_ref, mask_ref, embed_ref):
    chosen = column_of(mask_ref[...].astype(F32))
    return jnp.where(
        chosen > 0.5, embed_ref[...].astype(F32).reshape(1, D), patches_ref[0].astype(F32)
    )

def remote(src, dst, send, recv, k, where):
    return pltpu.make_async_remote_copy(
        src_ref=src,
        dst_ref=dst,
        send_sem=send.at[k],
        recv_sem=recv.at[k],
        device_id=where,
        device_id_type=MESH,
    )


def ring_of_four(own, ref_of, pos, parts, send, recv, to):
    first, second = parts
    before, after = lax.rem(pos + 3, 4), lax.rem(pos + 1, 4)

    def fresh(part, k, where):
        return remote(own(part), ref_of(pos, part), send, recv, k, where)

    def again(slot, part, k, where):
        ref = ref_of(slot, part)
        return remote(ref, ref, send, recv, k, where)

    return [
        fresh(first, 0, to(1)),
        fresh(second, 1, to(3)),
        fresh(second, 2, to(1)),
        fresh(first, 3, to(3)),
        again(before, first, 4, to(1)),
        again(after, second, 5, to(3)),
    ]


class PackRing:
    def __init__(self, n_pack, ref_of, limits, sems, base, own=None):
        self.p = lax.axis_index("pack")
        self.nz = n_pack // 2
        self.z, self.core = self.p // 2, lax.rem(self.p, 2)
        self.ref_of, self.limits, self.sems, self.base, self.own = ref_of, limits, sems, base, own
        self.made = {}

    def go(self, pack, step, k, own=False):
        z_send, z_recv, c_send, c_recv = self.sems
        ref = self.ref_of(pack)
        src = self.own if own and self.own is not None else ref
        if step == 2:
            to = self.z * 2 + 1 - self.core
            one = remote(src, ref, c_send, c_recv, self.base * self.nz + k, {"pack": to})
        else:
            to = lax.rem(self.z + step + self.nz, self.nz) * 2 + self.core
            n = (self.base * 2 + (step + 1) // 2) * self.nz + k
            one = remote(src, ref, z_send, z_recv, n, {"pack": to})
        one.start()
        self.made[step, k] = one

    def start(self):
        for step in (1, -1, 2):
            self.go(self.p, step, 0, own=True)

    def hop(self, h):
        for step, limit in ((1, self.limits[0]), (-1, self.limits[1])):
            if h > limit:
                continue
            self.made[step, h - 1].wait_recv()
            pack = lax.rem(self.z - step * h + self.nz, self.nz) * 2 + self.core
            if h < limit:
                self.go(pack, step, h)
            self.go(pack, 2, h if step == 1 else self.limits[0] + h)

    def finish(self):
        for k in range(self.nz):
            self.made[2, k].wait_recv()

    def drain(self):
        for one in self.made.values():
            one.wait_send()


def limits_of(nz, c):
    low, high = nz - 1 - nz // 2, nz // 2
    return (high, low) if c % 2 == 0 else (low, high)


def qkv_kernel(
    patches_ref,
    mask_ref,
    embed_ref,
    gain_ref,
    weight_ref,
    seg_ref,
    row_ref,
    col_ref,
    out_ref,
    labels_ref,
    tok,
    wts,
    prod,
    mine,
    t_send,
    t_recv,
    w_send,
    w_recv,
    p_send,
    p_recv,
    m_send,
    m_recv,
):
    s = lax.axis_index("seq")
    core = lax.rem(lax.axis_index("pack"), 2)
    y, x = s // 4, lax.rem(s, 4)
    a = x * (1 - core) + y * core
    b = y * (1 - core) + x * core
    step_a, step_b = 1 + 3 * core, 4 - 3 * core

    def on_a(k):
        return {"seq": lax.rem(a + k, 4) * step_a + b * step_b}

    def on_b(k):
        return {"seq": a * step_a + lax.rem(b + k, 4) * step_b}

    barrier = pltpu.get_barrier_semaphore()

    def greet(where):
        pl.semaphore_signal(barrier, inc=1, device_id=where, device_id_type=MESH)

    for d in range(1, 16):
        greet({"seq": lax.rem(s + d, 16)})

    mine[0:1, :] = seg_ref[...]
    mine[1:2, :] = row_ref[...]
    mine[2:3, :] = col_ref[...]
    mine[3:8, :] = jnp.zeros((5, ROWS), jnp.int32)
    labels_ref[s] = mine[...]
    pl.semaphore_wait(barrier, 15)

    w_ring = ring_of_four(
        lambda part: weight_ref.at[part],
        lambda slot, part: wts.at[slot, part],
        b,
        (pl.ds(0, 136), pl.ds(136, 128)),
        w_send,
        w_recv,
        on_b,
    )
    t_ring = ring_of_four(
        lambda part: tok.at[a, part],
        lambda slot, part: tok.at[slot, part],
        a,
        (pl.ds(0, 96), pl.ds(96, 96)),
        t_send,
        t_recv,
        on_a,
    )
    w_ring[0].start()
    w_ring[1].start()
    small = []
    for d in range(1, 16):
        small.append(
            remote(mine, labels_ref.at[s], m_send, m_recv, d, {"seq": lax.rem(s + d, 16)})
        )
    for one in small:
        one.start()
    w_ring[2].start()
    w_ring[3].start()
    inputs = embedded(patches_ref, mask_ref, embed_ref)
    tok[a] = layer_norm(inputs, gain_ref[...].astype(F32).reshape(1, D)).astype(BF16)
    for k in range(4):
        t_ring[k].start()
    wts[b] = weight_ref[...]
    for one in small:
        one.wait_recv()

    feature = iota((HD, 1), 0)
    quarter = HD // 4
    place = lax.rem(feature, quarter).astype(F32)
    frequency = jnp.exp(place * (-9.210340371976184 / quarter))
    is_row = feature < 2 * quarter
    is_first = lax.rem(feature, 2 * quarter) < quarter

    def table(pair):
        left = labels_ref[(2 * pair) * step_a + b * step_b].astype(F32)
        right = labels_ref[(2 * pair + 1) * step_a + b * step_b].astype(F32)
        both = side_by_side(left, right)
        angle = jnp.where(is_row, both[1:2], both[2:3]) * frequency
        sine = jnp.sin(angle)
        return jnp.cos(angle), jnp.where(is_first, -sine, 0.0), jnp.where(is_first, 0.0, sine)

    pairs = (a // 2, 1 - a // 2)
    tables = [table(pair) for pair in pairs]

    t_ring[0].wait_recv()
    t_ring[4].start()
    t_ring[1].wait_recv()
    t_ring[5].start()
    w_ring[0].wait_recv()
    w_ring[4].start()
    w_ring[1].wait_recv()
    w_ring[5].start()
    t_ring[2].wait_recv()
    t_ring[3].wait_recv()

    def turn(part, k):
        cosine, ahead, behind = tables[k]
        return (
            part * cosine
            + pltpu.roll(part, HD - quarter, 0) * ahead
            + pltpu.roll(part, quarter, 0) * behind
        )

    def block(k, head):
        tokens = tok[pl.ds(2 * pairs[k], 2)].reshape(2 * ROWS, D)
        projected = lax.dot_general(wts[head], tokens, NT, preferred_element_type=F32)
        return jnp.concatenate(
            [turn(projected[:HD], k), turn(projected[HD : 2 * HD], k), projected[2 * HD :]],
            axis=0,
        ).astype(BF16)

    sends = []

    def send_to(k, off):
        n = len(sends)
        prod[n] = block(k, lax.rem(b + off, 4))
        sends.append(remote(prod.at[n], out_ref.at[b, pairs[k]], p_send, p_recv, n, on_b(off)))
        sends[n].start()

    out_ref[b, pairs[0]] = block(0, b)
    w_ring[2].wait_recv()
    w_ring[3].wait_recv()
    send_to(0, 1)
    send_to(0, 3)
    t_ring[4].wait_recv()
    t_ring[5].wait_recv()
    send_to(1, 1)
    send_to(1, 3)
    w_ring[4].wait_recv()
    w_ring[5].wait_recv()
    send_to(0, 2)
    send_to(1, 2)
    out_ref[b, pairs[1]] = block(1, b)
    for one in sends:
        one.wait_recv()
    for one in w_ring + t_ring + small + sends:
        one.wait_send()


def attention_kernel(n_pack, qkv_ref, labels_ref, owner_ref, out_ref, table_ref, qs, kvs, segs):
    core = lax.rem(lax.axis_index("pack"), 2)
    half = ROWS
    wide = 2 * ROWS

    @pl.when(core == 0)
    def _():
        for m in range(8):
            kvs[m] = qkv_ref[m // 2, m % 2]

    @pl.when(core == 1)
    def _():
        lane = iota((3 * HD, wide), 1)
        for m in range(8):
            second, j = (m // 2) % 2, m // 4
            left = qkv_ref[2 * (m % 2), j].astype(F32)
            right = qkv_ref[2 * (m % 2) + 1, j].astype(F32)
            if second:
                left = pltpu.roll(left, half, 1)
            else:
                right = pltpu.roll(right, half, 1)
            kvs[m] = jnp.where(lane < half, left, right).astype(BF16)

    for m in range(8):
        turned = jnp.concatenate(
            [kvs[m].astype(F32)[:HD], jnp.zeros((128 - HD, wide), F32)], axis=0
        ).T
        qs[2 * m] = turned[:half].astype(BF16)
        qs[2 * m + 1] = turned[half:].astype(BF16)
        segs[m] = side_by_side(
            labels_ref[2 * m].astype(F32), labels_ref[2 * m + 1].astype(F32)
        )

    every = jnp.concatenate([labels_ref[k][0:1] for k in range(16)], axis=0)
    total = 16 * ROWS
    starts = [jnp.int32(0)]
    for image in range(1, 8):
        starts.append(jnp.sum((every < image).astype(jnp.int32)))
    starts.append(jnp.int32(total))
    lane = iota((1, 128), 1)
    first = jnp.zeros((1, 128), jnp.int32)
    length = jnp.zeros((1, 128), jnp.int32)
    for image in range(8):
        mine = lane == owner_ref[0, image]
        first = jnp.where(mine, starts[image] // 4, first)
        length = jnp.where(mine, (starts[image + 1] - starts[image]) // 4, length)
    table_ref[0:1, :] = first
    table_ref[1:2, :] = length
    table_ref[2:8, :] = jnp.zeros((6, 128), jnp.int32)

    scale = HD ** (-0.5) * 1.4426950408889634
    low = -0.7 * 3.4028235e38

    def one_block(s, carry):
        begin = jnp.int32(0)
        end = jnp.int32(total)
        for image in range(1, 8):
            begin = jnp.where(starts[image] <= s * ROWS, starts[image], begin)
        for image in range(7, 0, -1):
            end = jnp.where(starts[image] >= (s + 1) * ROWS, starts[image], end)
        queries = qs[s][:, :HD]
        own = column_of(labels_ref[s][0:1].astype(F32))

        def one_step(m, state):
            top, denominator, acc = state
            scores = jnp.dot(queries, kvs[m, pl.ds(HD, HD)], preferred_element_type=F32)
            scores = jnp.where(own == segs[m][0:1], scores, low)
            new_top = jnp.maximum(top, jnp.max(scores, axis=-1, keepdims=True))
            shrink = jnp.exp2((top - new_top) * scale)
            weights = jnp.exp2((scores - new_top) * scale)
            denominator = denominator * shrink + jnp.sum(weights, axis=-1, keepdims=True)
            acc = acc * shrink + lax.dot_general(
                weights.astype(BF16), kvs[m, pl.ds(2 * HD, HD)], NT, preferred_element_type=F32
            )
            return new_top, denominator, acc

        state = (
            jnp.full((ROWS, 1), low, F32),
            jnp.zeros((ROWS, 1), F32),
            jnp.zeros((ROWS, HD), F32),
        )
        _, denominator, acc = lax.fori_loop(
            begin // wide, (end + wide - 1) // wide, one_step, state
        )
        out_ref[s, :, :HD] = (acc / denominator).astype(BF16)
        out_ref[s, :, HD:] = jnp.zeros((ROWS, 128 - HD), BF16)
        return carry

    lax.fori_loop(0, 16, one_block, 0)


def merge_kernel(
    n_pack,
    att_ref,
    patches_ref,
    mask_ref,
    embed_ref,
    wo_ref,
    gain_ref,
    wm_ref,
    bias_ref,
    table_ref,
    rows_ref,
    tables_ref,
    heads,
    acc,
    tiles,
    mg,
    wv,
    l_sem,
    h_send,
    h_recv,
    g_send,
    g_recv,
    b_send,
    b_recv,
    z_send,
    z_recv,
    c_send,
    c_recv,
):
    s = lax.axis_index("seq")
    p = lax.axis_index("pack")
    nz = n_pack // 2
    y, x = s // 4, lax.rem(s, 4)

    barrier = pltpu.get_barrier_semaphore()
    for d in range(1, 16):
        pl.semaphore_signal(
            barrier, inc=1, device_id={"seq": lax.rem(s + d, 16)}, device_id_type=MESH
        )
    for d in range(1, n_pack):
        pl.semaphore_signal(
            barrier, inc=1, device_id={"pack": lax.rem(p + d, n_pack)}, device_id_type=MESH
        )
    load = pltpu.make_async_copy(wm_ref, wv, l_sem)
    load.start()
    tables_ref[p] = table_ref[...]
    rows_ref[p, :, :, OUTC:] = jnp.zeros((4, 4 * GROUPS, 256 - OUTC), BF16)
    pl.semaphore_wait(barrier, 15 + n_pack - 1)

    out = []
    back = []
    for d in range(1, 16):
        to = lax.rem(s + d, 16)
        back.append(remote(att_ref.at[to], heads.at[s], h_send, h_recv, d, {"seq": to}))
        back[-1].start()
    tabs = []
    for d in range(1, n_pack):
        tabs.append(
            remote(table_ref, tables_ref.at[p], b_send, b_recv, d, {"pack": lax.rem(p + d, n_pack)})
        )
        tabs[-1].start()
    out += back + tabs
    inputs = embedded(patches_ref, mask_ref, embed_ref)
    acc[...] = inputs + jnp.dot(
        att_ref[s][:, :HD], wo_ref[s], preferred_element_type=F32
    )
    for d in range(1, 16):
        back[d - 1].wait_recv()
        head = lax.rem(s + 16 - d, 16)
        acc[...] += jnp.dot(heads[head][:, :HD], wo_ref[head], preferred_element_type=F32)
    normed = layer_norm(acc[...], gain_ref[...].astype(F32).reshape(1, D))
    for t in range(D // 128):
        tiles[t] = normed[:, 128 * t : 128 * (t + 1)]
    for t in range(D // 128):
        for j in range(4):
            mg[s, j, :, 128 * t : 128 * (t + 1)] = tiles[t, pl.ds(j, GROUPS, stride=4), :].astype(
                BF16
            )

    order = {0: 0, -1: 1, 1: 2, 2: 3}

    def device(half, df, dg):
        dx, dy = (df, dg) if half == 0 else (dg, df)
        return lax.rem(y + dy + 4, 4) * 4 + lax.rem(x + dx + 4, 4)

    started = {}

    def send(half, phase, df, dg, kind):
        k = ((half * 2 + phase) * 4 + (order[df] if phase else 0)) * 4 + kind
        blk = device(half, df, dg)
        step = 1 if kind in (0, 2) else -1
        to = device(half, 0, step) if phase else device(half, step, 0)
        if kind < 2:
            ref = mg.at[blk, pl.ds(2 * half, 2)]
        else:
            ref = mg.at[blk, pl.ds(2 * half + kind - 2, 1)]
        one = remote(ref, ref, g_send, g_recv, k, {"seq": to})
        one.start()
        started[half, phase, order[df] if phase else 0, kind] = one
        out.append(one)

    def arrive(half, df, dg):
        phase = 0 if dg == 0 else 1
        off = df if phase == 0 else dg
        k = order[df] if phase else 0
        if off == 2:
            started[half, phase, k, 2].wait_recv()
            started[half, phase, k, 3].wait_recv()
        elif off == -1:
            started[half, phase, k, 0].wait_recv()
            send(half, phase, df, dg, 2)
        else:
            started[half, phase, k, 1].wait_recv()
            send(half, phase, df, dg, 3)
        if phase == 0:
            send(half, 1, df, 0, 0)
            send(half, 1, df, 0, 1)

    done = set()

    def need(half, df, dg):
        if (half, df, dg) not in done and (df, dg) != (0, 0):
            done.add((half, df, dg))
            arrive(half, df, dg)

    z_rings = []

    def launch(row, part):
        one = PackRing(
            n_pack,
            lambda pack: rows_ref.at[pack, row, part],
            limits_of(nz, len(z_rings)),
            (z_send, z_recv, c_send, c_recv),
            len(z_rings),
        )
        one.start()
        z_rings.append(one)

    def chunk(dy, pieces):
        row = lax.rem(y + dy + 4, 4)
        total = jnp.broadcast_to(
            bias_ref[...].astype(F32).reshape(1, OUTC), (4 * GROUPS, OUTC)
        )
        for j in range(4):
            part = mg[pl.ds(4 * row, 4), j].reshape(4 * GROUPS, D)
            total += lax.dot_general(
                part, wv[:, pl.ds(j * D, D)], NT, preferred_element_type=F32
            )
        rows_ref[p, row, :, :OUTC] = total.astype(BF16)
        size = 4 * GROUPS // pieces
        for n in range(pieces):
            launch(row, pl.ds(n * size, size))

    def hop(*which):
        for c, h in which:
            if h <= nz // 2:
                z_rings[c].hop(h)

    for half in range(2):
        send(half, 0, 0, 0, 0)
        send(half, 0, 0, 0, 1)
    for half in range(2):
        send(half, 1, 0, 0, 0)
        send(half, 1, 0, 0, 1)
    for half in range(2):
        need(half, -1, 0)
        need(half, 1, 0)
    for half in range(2):
        need(half, 0, -1)
        need(half, 0, 1)
    for half in range(2):
        need(half, 2, 0)

    def row_ready(dy):
        for dx in (0, -1, 1, 2):
            need(0, dx, dy)
            need(1, dy, dx)

    row_ready(0)
    load.wait()
    chunk(0, 1)
    for df in (-1, 1, 2):
        for dg in (-1, 1):
            for half in range(2):
                need(half, df, dg)
    hop((0, 1))
    row_ready(-1)
    chunk(-1, 1)
    hop((0, 2))
    row_ready(1)
    chunk(1, 1)
    hop((0, 3), (1, 1), (2, 1), (0, 4), (1, 2), (2, 2), (1, 3), (2, 3))
    row_ready(2)
    chunk(2, 2)
    hop((1, 4), (2, 4))
    for h in range(1, nz // 2 + 1):
        hop((3, h), (4, h))
    for one in z_rings:
        one.finish()
        one.drain()
    for one in tabs:
        one.wait_recv()
    for one in out:
        one.wait_send()


def select_kernel(n_pack, rows_ref, tables_ref, out_ref):
    p = lax.axis_index("pack")
    total = 4 * MOST
    window = MOST + 16
    for q in range(n_pack):
        mine = iota((1, 128), 1) == p
        first = jnp.sum(jnp.where(mine, tables_ref[q, 0:1, :], 0))
        length = jnp.sum(jnp.where(mine, tables_ref[q, 1:2, :], 0))
        base = pl.multiple_of(jnp.minimum((first // 16) * 16, total - window), 16)
        slot = iota((MOST, window), 0)
        source = iota((MOST, window), 1)
        pick = ((source == slot + (first - base)) & (slot < length)).astype(BF16)
        out_ref[0, q] = jnp.dot(
            pick, rows_ref[q, pl.ds(base, window)], preferred_element_type=F32
        )[:, :OUTC].astype(BF16)


def local(
    patches,
    patch_mask,
    mask_embed,
    norm_gain,
    qkv_weight,
    segment_ids,
    patch_rows,
    patch_column,
    out_weight,
    merge_gain,
    merge_weight,
    merge_bias,
    image_owner,
):
    n_pack = lax.axis_size("pack")
    nz = n_pack // 2
    dma = pltpu.SemaphoreType.DMA
    shape = jax.ShapeDtypeStruct
    embed = mask_embed
    wm = merge_weight.T
    qkv, labels = pl.pallas_call(
        qkv_kernel,
        out_shape=(
            shape((4, 2, 3 * HD, 2 * ROWS), BF16),
            shape((16, 8, ROWS), jnp.int32),
        ),
        in_specs=[VM] * 8,
        out_specs=(VM, VM),
        scratch_shapes=[
            pltpu.VMEM((4, ROWS, D), BF16),
            pltpu.VMEM((4, 3 * HD, D), BF16),
            pltpu.VMEM((6, 3 * HD, 2 * ROWS), BF16),
            pltpu.VMEM((8, ROWS), jnp.int32),
            dma((6,)),
            dma((6,)),
            dma((6,)),
            dma((6,)),
            dma((6,)),
            dma((6,)),
            dma((16,)),
            dma((16,)),
        ],
        compiler_params=pltpu.CompilerParams(
            collective_id=0, has_side_effects=True, vmem_limit_bytes=60 * 2**20
        ),
        name="qkv",
    )(
        patches,
        patch_mask,
        embed,
        norm_gain,
        qkv_weight.T,
        segment_ids,
        patch_rows,
        patch_column,
    )
    attended, table = pl.pallas_call(
        functools.partial(attention_kernel, n_pack),
        out_shape=(shape((16, ROWS, 128), BF16), shape((8, 128), jnp.int32)),
        in_specs=[VM, VM, SM],
        out_specs=(VM, VM),
        scratch_shapes=[
            pltpu.VMEM((16, ROWS, 128), BF16),
            pltpu.VMEM((8, 3 * HD, 2 * ROWS), BF16),
            pltpu.VMEM((8, 8, 2 * ROWS), F32),
        ],
        compiler_params=pltpu.CompilerParams(vmem_limit_bytes=60 * 2**20),
        name="attention",
    )(qkv, labels, image_owner)
    rows, tables = pl.pallas_call(
        functools.partial(merge_kernel, n_pack),
        out_shape=(
            shape((n_pack, 4, 4 * GROUPS, 256), BF16),
            shape((n_pack, 8, 128), jnp.int32),
        ),
        in_specs=[VM] * 6 + [ANY, VM, VM],
        out_specs=(VM, VM),
        scratch_shapes=[
            pltpu.VMEM((16, ROWS, 128), BF16),
            pltpu.VMEM((ROWS, D), F32),
            pltpu.VMEM((D // 128, ROWS, 128), F32),
            pltpu.VMEM((16, 4, GROUPS, D), BF16),
            pltpu.VMEM((OUTC, 4 * D), BF16),
            dma,
            dma((16,)),
            dma((16,)),
            dma((64,)),
            dma((64,)),
            dma((n_pack,)),
            dma((n_pack,)),
            dma((10 * nz,)),
            dma((10 * nz,)),
            dma((5 * nz,)),
            dma((5 * nz,)),
        ],
        compiler_params=pltpu.CompilerParams(
            collective_id=1, has_side_effects=True, vmem_limit_bytes=60 * 2**20
        ),
        name="merge",
    )(
        attended,
        patches,
        patch_mask,
        embed,
        out_weight.reshape(HEADS, HD, D),
        merge_gain,
        wm,
        merge_bias,
        table,
    )
    return pl.pallas_call(
        functools.partial(select_kernel, n_pack),
        out_shape=shape((1, n_pack, MOST, OUTC), BF16),
        in_specs=[VM, VM],
        out_specs=VM,
        compiler_params=pltpu.CompilerParams(vmem_limit_bytes=60 * 2**20),
        name="select",
    )(rows.reshape(n_pack, 4 * MOST, 256), tables)


def solution(mesh):
    placed = (
        P("pack", "seq", None),
        P("pack", "seq"),
        P(),
        P(),
        P(None, "seq"),
        P("pack", "seq"),
        P("pack", "seq"),
        P("pack", "seq"),
        P(),
        P(),
        P(None, "seq"),
        P("seq"),
        P("pack", None),
    )
    return jax.shard_map(
        local, mesh=mesh, in_specs=placed, out_specs=P("pack", None, None, "seq"), check_vma=False
    )
```

```python
import functools

import jax
import jax.numpy as jnp
from jax import lax
from jax.experimental import pallas as pl
from jax.experimental.pallas import tpu as pltpu
from jax.sharding import PartitionSpec as P

D = 1408
HEADS = 16
HD = 88
ROWS = 192
GROUPS = 48
OUTC = 224
MOST = 192
EPSILON = 1e-06
F32 = jnp.float32
BF16 = jnp.bfloat16
MESH = pl.DeviceIdType.MESH
NT = (((1,), (1,)), ((), ()))
VM = pl.BlockSpec(memory_space=pltpu.VMEM)
ANY = pl.BlockSpec(memory_space=pl.ANY)
SM = pl.BlockSpec(memory_space=pltpu.SMEM)


def iota(shape, axis):
    return lax.broadcasted_iota(jnp.int32, shape, axis)


def column_of(row):
    n = row.shape[1]
    eye = (iota((n, n), 0) == iota((n, n), 1)).astype(BF16)
    wide = jnp.broadcast_to(row, (8, n)).astype(BF16)
    return lax.dot_general(eye, wide, NT, preferred_element_type=F32)[:, :1]


def side_by_side(left, right):
    n = left.shape[1]
    first = (iota((n, 2 * n), 0) == iota((n, 2 * n), 1)).astype(BF16)
    second = (iota((n, 2 * n), 0) + n == iota((n, 2 * n), 1)).astype(BF16)
    return jnp.dot(left.astype(BF16), first, preferred_element_type=F32) + jnp.dot(
        right.astype(BF16), second, preferred_element_type=F32
    )


def layer_norm(values, gain):
    center = values - jnp.mean(values, axis=-1, keepdims=True)
    spread = jnp.mean(center * center, axis=-1, keepdims=True)
    return center * lax.rsqrt(spread + EPSILON) * gain


def embedded(patches_ref, mask_ref, embed_ref):
    chosen = column_of(mask_ref[...].astype(F32))
    return jnp.where(
        chosen > 0.5, embed_ref[...].astype(F32).reshape(1, D), patches_ref[0].astype(F32)
    )

def remote(src, dst, send, recv, k, where):
    return pltpu.make_async_remote_copy(
        src_ref=src,
        dst_ref=dst,
        send_sem=send.at[k],
        recv_sem=recv.at[k],
        device_id=where,
        device_id_type=MESH,
    )


def ring_of_four(own, ref_of, pos, parts, send, recv, to):
    first, second = parts
    before, after = lax.rem(pos + 3, 4), lax.rem(pos + 1, 4)

    def fresh(part, k, where):
        return remote(own(part), ref_of(pos, part), send, recv, k, where)

    def again(slot, part, k, where):
        ref = ref_of(slot, part)
        return remote(ref, ref, send, recv, k, where)

    return [
        fresh(first, 0, to(1)),
        fresh(second, 1, to(3)),
        fresh(second, 2, to(1)),
        fresh(first, 3, to(3)),
        again(before, first, 4, to(1)),
        again(after, second, 5, to(3)),
    ]


class PackRing:
    def __init__(self, n_pack, ref_of, limits, sems, base, own=None):
        self.p = lax.axis_index("pack")
        self.nz = n_pack // 2
        self.z, self.core = self.p // 2, lax.rem(self.p, 2)
        self.ref_of, self.limits, self.sems, self.base, self.own = ref_of, limits, sems, base, own
        self.made = {}

    def go(self, pack, step, k, own=False):
        z_send, z_recv, c_send, c_recv = self.sems
        ref = self.ref_of(pack)
        src = self.own if own and self.own is not None else ref
        if step == 2:
            to = self.z * 2 + 1 - self.core
            one = remote(src, ref, c_send, c_recv, self.base * self.nz + k, {"pack": to})
        else:
            to = lax.rem(self.z + step + self.nz, self.nz) * 2 + self.core
            n = (self.base * 2 + (step + 1) // 2) * self.nz + k
            one = remote(src, ref, z_send, z_recv, n, {"pack": to})
        one.start()
        self.made[step, k] = one

    def start(self):
        for step in (1, -1, 2):
            self.go(self.p, step, 0, own=True)

    def hop(self, h):
        for step, limit in ((1, self.limits[0]), (-1, self.limits[1])):
            if h > limit:
                continue
            self.made[step, h - 1].wait_recv()
            pack = lax.rem(self.z - step * h + self.nz, self.nz) * 2 + self.core
            if h < limit:
                self.go(pack, step, h)
            self.go(pack, 2, h if step == 1 else self.limits[0] + h)

    def finish(self):
        for k in range(self.nz):
            self.made[2, k].wait_recv()

    def drain(self):
        for one in self.made.values():
            one.wait_send()


ORDER = (
    (0, 0), (-1, 0), (1, 0), (0, -1), (0, 1),
    (2, 0), (0, 2),
    (-1, -1), (1, -1), (-1, 1), (1, 1),
    (2, -1), (2, 1), (-1, 2), (1, 2), (2, 2),
)


def limits_of(nz, c):
    low, high = nz - 1 - nz // 2, nz // 2
    return (high, low) if c % 2 == 0 else (low, high)


def qkv_kernel(
    patches_ref,
    mask_ref,
    embed_ref,
    gain_ref,
    weight_ref,
    seg_ref,
    row_ref,
    col_ref,
    out_ref,
    labels_ref,
    tok,
    wts,
    prod,
    mine,
    t_send,
    t_recv,
    w_send,
    w_recv,
    p_send,
    p_recv,
    m_send,
    m_recv,
):
    s = lax.axis_index("seq")
    core = lax.rem(lax.axis_index("pack"), 2)
    y, x = s // 4, lax.rem(s, 4)
    a = x * (1 - core) + y * core
    b = y * (1 - core) + x * core
    step_a, step_b = 1 + 3 * core, 4 - 3 * core

    def on_a(k):
        return {"seq": lax.rem(a + k, 4) * step_a + b * step_b}

    def on_b(k):
        return {"seq": a * step_a + lax.rem(b + k, 4) * step_b}

    barrier = pltpu.get_barrier_semaphore()

    def greet(where):
        pl.semaphore_signal(barrier, inc=1, device_id=where, device_id_type=MESH)

    for d in range(1, 16):
        greet({"seq": lax.rem(s + d, 16)})

    mine[0:1, :] = seg_ref[...]
    mine[1:2, :] = row_ref[...]
    mine[2:3, :] = col_ref[...]
    mine[3:8, :] = jnp.zeros((5, ROWS), jnp.int32)
    labels_ref[s] = mine[...]
    pl.semaphore_wait(barrier, 15)

    w_ring = ring_of_four(
        lambda part: weight_ref.at[part],
        lambda slot, part: wts.at[slot, part],
        b,
        (pl.ds(0, 136), pl.ds(136, 128)),
        w_send,
        w_recv,
        on_b,
    )
    t_ring = ring_of_four(
        lambda part: tok.at[a, part],
        lambda slot, part: tok.at[slot, part],
        a,
        (pl.ds(0, 96), pl.ds(96, 96)),
        t_send,
        t_recv,
        on_a,
    )
    w_ring[0].start()
    w_ring[1].start()
    small = []
    for d in range(1, 16):
        small.append(
            remote(mine, labels_ref.at[s], m_send, m_recv, d, {"seq": lax.rem(s + d, 16)})
        )
    for one in small:
        one.start()
    w_ring[2].start()
    w_ring[3].start()
    inputs = embedded(patches_ref, mask_ref, embed_ref)
    tok[a] = layer_norm(inputs, gain_ref[...].astype(F32).reshape(1, D)).astype(BF16)
    for k in range(4):
        t_ring[k].start()
    wts[b] = weight_ref[...]
    for one in small:
        one.wait_recv()

    feature = iota((HD, 1), 0)
    quarter = HD // 4
    place = lax.rem(feature, quarter).astype(F32)
    frequency = jnp.exp(place * (-9.210340371976184 / quarter))
    is_row = feature < 2 * quarter
    is_first = lax.rem(feature, 2 * quarter) < quarter

    def table(pair):
        left = labels_ref[(2 * pair) * step_a + b * step_b].astype(F32)
        right = labels_ref[(2 * pair + 1) * step_a + b * step_b].astype(F32)
        both = side_by_side(left, right)
        angle = jnp.where(is_row, both[1:2], both[2:3]) * frequency
        sine = jnp.sin(angle)
        return jnp.cos(angle), jnp.where(is_first, -sine, 0.0), jnp.where(is_first, 0.0, sine)

    pairs = (a // 2, 1 - a // 2)
    tables = [table(pair) for pair in pairs]

    t_ring[0].wait_recv()
    t_ring[4].start()
    t_ring[1].wait_recv()
    t_ring[5].start()
    w_ring[0].wait_recv()
    w_ring[4].start()
    w_ring[1].wait_recv()
    w_ring[5].start()
    t_ring[2].wait_recv()
    t_ring[3].wait_recv()

    def turn(part, k):
        cosine, ahead, behind = tables[k]
        return (
            part * cosine
            + pltpu.roll(part, HD - quarter, 0) * ahead
            + pltpu.roll(part, quarter, 0) * behind
        )

    def block(k, head):
        tokens = tok[pl.ds(2 * pairs[k], 2)].reshape(2 * ROWS, D)
        projected = lax.dot_general(wts[head], tokens, NT, preferred_element_type=F32)
        return jnp.concatenate(
            [turn(projected[:HD], k), turn(projected[HD : 2 * HD], k), projected[2 * HD :]],
            axis=0,
        ).astype(BF16)

    sends = []

    def send_to(k, off):
        n = len(sends)
        prod[n] = block(k, lax.rem(b + off, 4))
        sends.append(remote(prod.at[n], out_ref.at[b, pairs[k]], p_send, p_recv, n, on_b(off)))
        sends[n].start()

    out_ref[b, pairs[0]] = block(0, b)
    w_ring[2].wait_recv()
    w_ring[3].wait_recv()
    send_to(0, 1)
    send_to(0, 3)
    t_ring[4].wait_recv()
    t_ring[5].wait_recv()
    send_to(1, 1)
    send_to(1, 3)
    w_ring[4].wait_recv()
    w_ring[5].wait_recv()
    send_to(0, 2)
    send_to(1, 2)
    out_ref[b, pairs[1]] = block(1, b)
    for one in sends:
        one.wait_recv()
    for one in w_ring + t_ring + small + sends:
        one.wait_send()


def attention_kernel(n_pack, qkv_ref, labels_ref, owner_ref, out_ref, table_ref, kvs, segs, keys, marks, values):
    core = lax.rem(lax.axis_index("pack"), 2)
    half = ROWS
    wide = 2 * ROWS

    @pl.when(core == 0)
    def _():
        for m in range(8):
            kvs[m] = qkv_ref[m // 2, m % 2]

    @pl.when(core == 1)
    def _():
        lane = iota((3 * HD, wide), 1)
        for m in range(8):
            second, j = (m // 2) % 2, m // 4
            left = qkv_ref[2 * (m % 2), j].astype(F32)
            right = qkv_ref[2 * (m % 2) + 1, j].astype(F32)
            if second:
                left = pltpu.roll(left, half, 1)
            else:
                right = pltpu.roll(right, half, 1)
            kvs[m] = jnp.where(lane < half, left, right).astype(BF16)

    for m in range(8):
        segs[m] = side_by_side(
            labels_ref[2 * m].astype(F32), labels_ref[2 * m + 1].astype(F32)
        )
        fill = jnp.zeros((128 - HD, wide), F32)
        both = kvs[m].astype(F32)
        keys[m] = jnp.concatenate([both[HD : 2 * HD], fill], axis=0).T.astype(BF16)
        values[m] = jnp.concatenate([both[2 * HD :], fill], axis=0).astype(BF16)
        marks[m] = column_of(segs[m][0:1])

    every = jnp.concatenate([labels_ref[k][0:1] for k in range(16)], axis=0)
    total = 16 * ROWS
    starts = [jnp.int32(0)]
    for image in range(1, 8):
        starts.append(jnp.sum((every < image).astype(jnp.int32)))
    starts.append(jnp.int32(total))
    lane = iota((1, 128), 1)
    first = jnp.zeros((1, 128), jnp.int32)
    length = jnp.zeros((1, 128), jnp.int32)
    for image in range(8):
        mine = lane == owner_ref[0, image]
        first = jnp.where(mine, starts[image] // 4, first)
        length = jnp.where(mine, (starts[image + 1] - starts[image]) // 4, length)
    table_ref[0:1, :] = first
    table_ref[1:2, :] = length
    table_ref[2:8, :] = jnp.zeros((6, 128), jnp.int32)

    scale = HD ** (-0.5) * 1.4426950408889634
    low = -0.7 * 3.4028235e38

    size = 2 * wide

    def one_block(g, carry):
        begin = jnp.int32(0)
        end = jnp.int32(total)
        for image in range(1, 8):
            begin = jnp.where(starts[image] <= g * size, starts[image], begin)
        for image in range(7, 0, -1):
            end = jnp.where(starts[image] >= (g + 1) * size, starts[image], end)
        queries = jnp.concatenate(
            [kvs[2 * g, pl.ds(0, HD)], kvs[2 * g + 1, pl.ds(0, HD)]], axis=1
        )
        own = jnp.concatenate([segs[2 * g][0:1], segs[2 * g + 1][0:1]], axis=1)

        def one_step(m, state):
            top, denominator, acc = state
            scores = jnp.dot(keys[m][:, :HD], queries, preferred_element_type=F32)
            scores = jnp.where(marks[m] == own, scores, low)
            new_top = jnp.maximum(top, jnp.max(scores, axis=0, keepdims=True))
            shrink = jnp.exp2((top - new_top) * scale)
            weights = jnp.exp2((scores - new_top) * scale)
            denominator = denominator * shrink + jnp.sum(weights, axis=0, keepdims=True)
            acc = acc * shrink + jnp.dot(
                values[m], weights.astype(BF16), preferred_element_type=F32
            )
            return new_top, denominator, acc

        state = (
            jnp.full((1, size), low, F32),
            jnp.zeros((1, size), F32),
            jnp.zeros((128, size), F32),
        )
        _, denominator, acc = lax.fori_loop(
            begin // wide, (end + wide - 1) // wide, one_step, state
        )
        result = (acc / denominator).T
        for n in range(4):
            out_ref[4 * g + n] = result[n * ROWS : (n + 1) * ROWS].astype(BF16)
        return carry

    lax.fori_loop(0, total // size, one_block, 0)


def merge_kernel(
    n_pack,
    att_ref,
    patches_ref,
    mask_ref,
    embed_ref,
    wo_ref,
    gain_ref,
    wm_ref,
    bias_ref,
    table_ref,
    rows_ref,
    tables_ref,
    heads,
    acc,
    tiles,
    mg,
    wv,
    l_sem,
    h_send,
    h_recv,
    g_send,
    g_recv,
    b_send,
    b_recv,
    z_send,
    z_recv,
    c_send,
    c_recv,
):
    s = lax.axis_index("seq")
    p = lax.axis_index("pack")
    nz = n_pack // 2
    y, x = s // 4, lax.rem(s, 4)

    barrier = pltpu.get_barrier_semaphore()
    for d in range(1, 16):
        pl.semaphore_signal(
            barrier, inc=1, device_id={"seq": lax.rem(s + d, 16)}, device_id_type=MESH
        )
    for d in range(1, n_pack):
        pl.semaphore_signal(
            barrier, inc=1, device_id={"pack": lax.rem(p + d, n_pack)}, device_id_type=MESH
        )
    load = pltpu.make_async_copy(wm_ref, wv, l_sem)
    load.start()
    tables_ref[p] = table_ref[...]
    rows_ref[p, :, :, OUTC:] = jnp.zeros((16, GROUPS, 256 - OUTC), BF16)
    pl.semaphore_wait(barrier, 15 + n_pack - 1)

    out = []
    back = []
    for d in range(1, 16):
        to = lax.rem(s + d, 16)
        back.append(remote(att_ref.at[to], heads.at[s], h_send, h_recv, d, {"seq": to}))
        back[-1].start()
    tabs = []
    for d in range(1, n_pack):
        tabs.append(
            remote(table_ref, tables_ref.at[p], b_send, b_recv, d, {"pack": lax.rem(p + d, n_pack)})
        )
        tabs[-1].start()
    out += back + tabs
    inputs = embedded(patches_ref, mask_ref, embed_ref)
    acc[...] = inputs + jnp.dot(
        att_ref[s][:, :HD], wo_ref[s], preferred_element_type=F32
    )
    for d in range(1, 16):
        back[d - 1].wait_recv()
        head = lax.rem(s + 16 - d, 16)
        acc[...] += jnp.dot(heads[head][:, :HD], wo_ref[head], preferred_element_type=F32)
    normed = layer_norm(acc[...], gain_ref[...].astype(F32).reshape(1, D))
    for t in range(D // 128):
        tiles[t] = normed[:, 128 * t : 128 * (t + 1)]
    for t in range(D // 128):
        for j in range(4):
            mg[s, j, :, 128 * t : 128 * (t + 1)] = tiles[t, pl.ds(j, GROUPS, stride=4), :].astype(
                BF16
            )

    order = {0: 0, -1: 1, 1: 2, 2: 3}

    def device(half, df, dg):
        dx, dy = (df, dg) if half == 0 else (dg, df)
        return lax.rem(y + dy + 4, 4) * 4 + lax.rem(x + dx + 4, 4)

    started = {}

    def send(half, phase, df, dg, kind):
        k = ((half * 2 + phase) * 4 + (order[df] if phase else 0)) * 4 + kind
        blk = device(half, df, dg)
        step = 1 if kind in (0, 2) else -1
        to = device(half, 0, step) if phase else device(half, step, 0)
        if kind < 2:
            ref = mg.at[blk, pl.ds(2 * half, 2)]
        else:
            ref = mg.at[blk, pl.ds(2 * half + kind - 2, 1)]
        one = remote(ref, ref, g_send, g_recv, k, {"seq": to})
        one.start()
        started[half, phase, order[df] if phase else 0, kind] = one
        out.append(one)

    def arrive(half, df, dg):
        phase = 0 if dg == 0 else 1
        off = df if phase == 0 else dg
        k = order[df] if phase else 0
        if off == 2:
            started[half, phase, k, 2].wait_recv()
            started[half, phase, k, 3].wait_recv()
        elif off == -1:
            started[half, phase, k, 0].wait_recv()
            send(half, phase, df, dg, 2)
        else:
            started[half, phase, k, 1].wait_recv()
            send(half, phase, df, dg, 3)
        if phase == 0:
            send(half, 1, df, 0, 0)
            send(half, 1, df, 0, 1)

    done = set()

    def need(half, df, dg):
        if (half, df, dg) not in done and (df, dg) != (0, 0):
            done.add((half, df, dg))
            arrive(half, df, dg)

    z_rings = []

    def launch(first, count):
        one = PackRing(
            n_pack,
            lambda pack: rows_ref.at[pack, pl.ds(first, count)],
            limits_of(nz, len(z_rings)),
            (z_send, z_recv, c_send, c_recv),
            len(z_rings),
        )
        one.start()
        z_rings.append(one)

    def chunk(first, count, pieces):
        blocks = ORDER[first : first + count]
        total = jnp.broadcast_to(
            bias_ref[...].astype(F32).reshape(1, OUTC), (count * GROUPS, OUTC)
        )
        for dx, dy in blocks:
            need(0, dx, dy)
            need(1, dy, dx)
        for j in range(4):
            part = jnp.concatenate([mg[device(0, dx, dy), j] for dx, dy in blocks], axis=0)
            total += lax.dot_general(
                part, wv[:, pl.ds(j * D, D)], NT, preferred_element_type=F32
            )
        total = total.astype(BF16)
        for n in range(count):
            rows_ref[p, first + n, :, :OUTC] = total[n * GROUPS : (n + 1) * GROUPS]
        for n in pieces:
            launch(first, n)
            first += n

    def hop(*which):
        for c, h in which:
            if h <= nz // 2:
                z_rings[c].hop(h)

    for half in range(2):
        send(half, 0, 0, 0, 0)
        send(half, 0, 0, 0, 1)
    for half in range(2):
        send(half, 1, 0, 0, 0)
        send(half, 1, 0, 0, 1)
    for half in range(2):
        need(half, -1, 0)
        need(half, 1, 0)
    for half in range(2):
        need(half, 0, -1)
        need(half, 0, 1)
    load.wait()
    chunk(0, 5, (5,))
    for half in range(2):
        need(half, 2, 0)
    chunk(5, 2, (2,))
    hop((0, 1))
    for df in (-1, 1):
        for half in range(2):
            need(half, df, -1)
            need(half, df, 1)
        hop((0, 2), (1, 1)) if df == -1 else hop((0, 3), (1, 2))
    chunk(7, 4, (4,))
    for half in range(2):
        need(half, 2, -1)
        need(half, 2, 1)
    hop((0, 4), (1, 3), (1, 4), (2, 1), (2, 2))
    chunk(11, 5, (3, 2))
    hop((2, 3), (3, 1), (4, 1), (2, 4))
    for h in range(2, nz // 2 + 1):
        hop((3, h), (4, h))
    for one in z_rings:
        one.finish()
        one.drain()
    for one in tabs:
        one.wait_recv()
    for one in out:
        one.wait_send()


def select_kernel(n_pack, arrived_ref, tables_ref, out_ref, rows, sems):
    p = lax.axis_index("pack")
    s = lax.axis_index("seq")
    y, x = s // 4, lax.rem(s, 4)
    loads = []
    for n, (dx, dy) in enumerate(ORDER):
        place = lax.rem(y + dy + 4, 4) * 4 + lax.rem(x + dx + 4, 4)
        start = pl.multiple_of(place * GROUPS, GROUPS)
        loads.append(
            pltpu.make_async_copy(
                arrived_ref.at[:, n], rows.at[:, pl.ds(start, GROUPS)], sems.at[n]
            )
        )
        loads[-1].start()
    for one in loads:
        one.wait()
    total = 4 * MOST
    window = MOST + 16
    for q in range(n_pack):
        mine = iota((1, 128), 1) == p
        first = jnp.sum(jnp.where(mine, tables_ref[q, 0:1, :], 0))
        length = jnp.sum(jnp.where(mine, tables_ref[q, 1:2, :], 0))
        base = pl.multiple_of(jnp.minimum((first // 16) * 16, total - window), 16)
        slot = iota((MOST, window), 0)
        source = iota((MOST, window), 1)
        pick = ((source == slot + (first - base)) & (slot < length)).astype(BF16)
        out_ref[0, q] = jnp.dot(
            pick, rows[q, pl.ds(base, window)], preferred_element_type=F32
        )[:, :OUTC].astype(BF16)


def local(
    patches,
    patch_mask,
    mask_embed,
    norm_gain,
    qkv_weight,
    segment_ids,
    patch_rows,
    patch_column,
    out_weight,
    merge_gain,
    merge_weight,
    merge_bias,
    image_owner,
):
    n_pack = lax.axis_size("pack")
    nz = n_pack // 2
    dma = pltpu.SemaphoreType.DMA
    shape = jax.ShapeDtypeStruct
    embed = mask_embed
    wm = merge_weight.T
    qkv, labels = pl.pallas_call(
        qkv_kernel,
        out_shape=(
            shape((4, 2, 3 * HD, 2 * ROWS), BF16),
            shape((16, 8, ROWS), jnp.int32),
        ),
        in_specs=[VM] * 8,
        out_specs=(VM, VM),
        scratch_shapes=[
            pltpu.VMEM((4, ROWS, D), BF16),
            pltpu.VMEM((4, 3 * HD, D), BF16),
            pltpu.VMEM((6, 3 * HD, 2 * ROWS), BF16),
            pltpu.VMEM((8, ROWS), jnp.int32),
            dma((6,)),
            dma((6,)),
            dma((6,)),
            dma((6,)),
            dma((6,)),
            dma((6,)),
            dma((16,)),
            dma((16,)),
        ],
        compiler_params=pltpu.CompilerParams(
            collective_id=0, has_side_effects=True, vmem_limit_bytes=60 * 2**20
        ),
        name="qkv",
    )(
        patches,
        patch_mask,
        embed,
        norm_gain,
        qkv_weight.T,
        segment_ids,
        patch_rows,
        patch_column,
    )
    attended, table = pl.pallas_call(
        functools.partial(attention_kernel, n_pack),
        out_shape=(shape((16, ROWS, 128), BF16), shape((8, 128), jnp.int32)),
        in_specs=[VM, VM, SM],
        out_specs=(VM, VM),
        scratch_shapes=[
            pltpu.VMEM((8, 3 * HD, 2 * ROWS), BF16),
            pltpu.VMEM((8, 8, 2 * ROWS), F32),
            pltpu.VMEM((8, 2 * ROWS, 128), BF16),
            pltpu.VMEM((8, 2 * ROWS, 1), F32),
            pltpu.VMEM((8, 128, 2 * ROWS), BF16),
        ],
        compiler_params=pltpu.CompilerParams(vmem_limit_bytes=60 * 2**20),
        name="attention",
    )(qkv, labels, image_owner)
    rows, tables = pl.pallas_call(
        functools.partial(merge_kernel, n_pack),
        out_shape=(
            shape((n_pack, 16, GROUPS, 256), BF16),
            shape((n_pack, 8, 128), jnp.int32),
        ),
        in_specs=[VM] * 6 + [ANY, VM, VM],
        out_specs=(VM, VM),
        scratch_shapes=[
            pltpu.VMEM((16, ROWS, 128), BF16),
            pltpu.VMEM((ROWS, D), F32),
            pltpu.VMEM((D // 128, ROWS, 128), F32),
            pltpu.VMEM((16, 4, GROUPS, D), BF16),
            pltpu.VMEM((OUTC, 4 * D), BF16),
            dma,
            dma((16,)),
            dma((16,)),
            dma((64,)),
            dma((64,)),
            dma((n_pack,)),
            dma((n_pack,)),
            dma((10 * nz,)),
            dma((10 * nz,)),
            dma((5 * nz,)),
            dma((5 * nz,)),
        ],
        compiler_params=pltpu.CompilerParams(
            collective_id=1, has_side_effects=True, vmem_limit_bytes=60 * 2**20
        ),
        name="merge",
    )(
        attended,
        patches,
        patch_mask,
        embed,
        out_weight.reshape(HEADS, HD, D),
        merge_gain,
        wm,
        merge_bias,
        table,
    )
    return pl.pallas_call(
        functools.partial(select_kernel, n_pack),
        out_shape=shape((1, n_pack, MOST, OUTC), BF16),
        in_specs=[ANY, VM],
        out_specs=VM,
        scratch_shapes=[pltpu.VMEM((n_pack, 4 * MOST, 256), BF16), dma((16,))],
        compiler_params=pltpu.CompilerParams(vmem_limit_bytes=60 * 2**20),
        name="select",
    )(rows, tables)


def solution(mesh):
    placed = (
        P("pack", "seq", None),
        P("pack", "seq"),
        P(),
        P(),
        P(None, "seq"),
        P("pack", "seq"),
        P("pack", "seq"),
        P("pack", "seq"),
        P(),
        P(),
        P(None, "seq"),
        P("seq"),
        P("pack", None),
    )
    return jax.shard_map(
        local, mesh=mesh, in_specs=placed, out_specs=P("pack", None, None, "seq"), check_vma=False
    )
```

```python
import functools

import jax
import jax.numpy as jnp
from jax import lax
from jax.experimental import pallas as pl
from jax.experimental.pallas import tpu as pltpu
from jax.sharding import PartitionSpec as P

D = 1408
HEADS = 16
HD = 88
ROWS = 192
GROUPS = 48
OUTC = 224
MOST = 192
EPSILON = 1e-06
F32 = jnp.float32
BF16 = jnp.bfloat16
MESH = pl.DeviceIdType.MESH
NT = (((1,), (1,)), ((), ()))
VM = pl.BlockSpec(memory_space=pltpu.VMEM)
ANY = pl.BlockSpec(memory_space=pl.ANY)
SM = pl.BlockSpec(memory_space=pltpu.SMEM)


def iota(shape, axis):
    return lax.broadcasted_iota(jnp.int32, shape, axis)


def column_of(row):
    n = row.shape[1]
    eye = (iota((n, n), 0) == iota((n, n), 1)).astype(BF16)
    wide = jnp.broadcast_to(row, (8, n)).astype(BF16)
    return lax.dot_general(eye, wide, NT, preferred_element_type=F32)[:, :1]


def side_by_side(left, right):
    n = left.shape[1]
    first = (iota((n, 2 * n), 0) == iota((n, 2 * n), 1)).astype(BF16)
    second = (iota((n, 2 * n), 0) + n == iota((n, 2 * n), 1)).astype(BF16)
    return jnp.dot(left.astype(BF16), first, preferred_element_type=F32) + jnp.dot(
        right.astype(BF16), second, preferred_element_type=F32
    )


def layer_norm(values, gain):
    center = values - jnp.mean(values, axis=-1, keepdims=True)
    spread = jnp.mean(center * center, axis=-1, keepdims=True)
    return center * lax.rsqrt(spread + EPSILON) * gain


def embedded(patches_ref, mask_ref, embed_ref):
    chosen = column_of(mask_ref[...].astype(F32))
    return jnp.where(
        chosen > 0.5, embed_ref[...].astype(F32).reshape(1, D), patches_ref[0].astype(F32)
    )

def remote(src, dst, send, recv, k, where):
    return pltpu.make_async_remote_copy(
        src_ref=src,
        dst_ref=dst,
        send_sem=send.at[k],
        recv_sem=recv.at[k],
        device_id=where,
        device_id_type=MESH,
    )


def ring_of_four(own, ref_of, pos, parts, send, recv, to):
    first, second = parts
    before, after = lax.rem(pos + 3, 4), lax.rem(pos + 1, 4)

    def fresh(part, k, where):
        return remote(own(part), ref_of(pos, part), send, recv, k, where)

    def again(slot, part, k, where):
        ref = ref_of(slot, part)
        return remote(ref, ref, send, recv, k, where)

    return [
        fresh(first, 0, to(1)),
        fresh(second, 1, to(3)),
        fresh(second, 2, to(1)),
        fresh(first, 3, to(3)),
        again(before, first, 4, to(1)),
        again(after, second, 5, to(3)),
    ]


class PackRing:
    def __init__(self, n_pack, ref_of, limits, sems, base, own=None):
        self.p = lax.axis_index("pack")
        self.nz = n_pack // 2
        self.z, self.core = self.p // 2, lax.rem(self.p, 2)
        self.ref_of, self.limits, self.sems, self.base, self.own = ref_of, limits, sems, base, own
        self.made = {}

    def go(self, pack, step, k, own=False):
        z_send, z_recv, c_send, c_recv = self.sems
        ref = self.ref_of(pack)
        src = self.own if own and self.own is not None else ref
        if step == 2:
            to = self.z * 2 + 1 - self.core
            one = remote(src, ref, c_send, c_recv, self.base * self.nz + k, {"pack": to})
        else:
            to = lax.rem(self.z + step + self.nz, self.nz) * 2 + self.core
            n = (self.base * 2 + (step + 1) // 2) * self.nz + k
            one = remote(src, ref, z_send, z_recv, n, {"pack": to})
        one.start()
        self.made[step, k] = one

    def start(self):
        for step in (1, -1, 2):
            self.go(self.p, step, 0, own=True)

    def hop(self, h):
        for step, limit in ((1, self.limits[0]), (-1, self.limits[1])):
            if h > limit:
                continue
            self.made[step, h - 1].wait_recv()
            pack = lax.rem(self.z - step * h + self.nz, self.nz) * 2 + self.core
            if h < limit:
                self.go(pack, step, h)
            self.go(pack, 2, h if step == 1 else self.limits[0] + h)

    def finish(self):
        for k in range(self.nz):
            self.made[2, k].wait_recv()

    def drain(self):
        for one in self.made.values():
            one.wait_send()


class PackDirect(PackRing):
    def start(self):
        z_send, z_recv, c_send, c_recv = self.sems
        ref = self.ref_of(self.p)
        self.go(self.p, 2, 0)
        steps = [k for n in range(1, self.nz // 2 + 1) for k in (n, self.nz - n)]
        for k in dict.fromkeys(steps):
            to = lax.rem(self.z + k, self.nz) * 2 + self.core
            one = remote(ref, ref, z_send, z_recv, self.base * 2 * self.nz + k, {"pack": to})
            one.start()
            self.made[1, k] = one

    def share(self):
        for k in range(1, self.nz):
            self.made[1, k].wait_recv()
            self.go(lax.rem(self.z - k + self.nz, self.nz) * 2 + self.core, 2, k)


ORDER = (
    (0, 0), (-1, 0), (1, 0), (0, -1), (0, 1),
    (2, 0), (0, 2),
    (-1, -1), (1, -1), (-1, 1), (1, 1),
    (2, -1), (2, 1), (-1, 2), (1, 2), (2, 2),
)


def limits_of(nz, c):
    low, high = nz - 1 - nz // 2, nz // 2
    return (high, low) if c % 2 == 0 else (low, high)


def qkv_kernel(
    patches_ref,
    mask_ref,
    embed_ref,
    gain_ref,
    weight_ref,
    seg_ref,
    row_ref,
    col_ref,
    out_ref,
    labels_ref,
    tok,
    wts,
    prod,
    mine,
    t_send,
    t_recv,
    w_send,
    w_recv,
    p_send,
    p_recv,
    m_send,
    m_recv,
):
    s = lax.axis_index("seq")
    core = lax.rem(lax.axis_index("pack"), 2)
    y, x = s // 4, lax.rem(s, 4)
    a = x * (1 - core) + y * core
    b = y * (1 - core) + x * core
    step_a, step_b = 1 + 3 * core, 4 - 3 * core

    def on_a(k):
        return {"seq": lax.rem(a + k, 4) * step_a + b * step_b}

    def on_b(k):
        return {"seq": a * step_a + lax.rem(b + k, 4) * step_b}

    barrier = pltpu.get_barrier_semaphore()

    def greet(where):
        pl.semaphore_signal(barrier, inc=1, device_id=where, device_id_type=MESH)

    for d in range(1, 16):
        greet({"seq": lax.rem(s + d, 16)})

    mine[0:1, :] = seg_ref[...]
    mine[1:2, :] = row_ref[...]
    mine[2:3, :] = col_ref[...]
    mine[3:8, :] = jnp.zeros((5, ROWS), jnp.int32)
    labels_ref[s] = mine[...]
    pl.semaphore_wait(barrier, 15)

    w_ring = ring_of_four(
        lambda part: weight_ref.at[part],
        lambda slot, part: wts.at[slot, part],
        b,
        (pl.ds(0, 136), pl.ds(136, 128)),
        w_send,
        w_recv,
        on_b,
    )
    t_ring = ring_of_four(
        lambda part: tok.at[a, part],
        lambda slot, part: tok.at[slot, part],
        a,
        (pl.ds(0, 96), pl.ds(96, 96)),
        t_send,
        t_recv,
        on_a,
    )
    w_ring[0].start()
    w_ring[1].start()
    small = []
    for d in range(1, 16):
        small.append(
            remote(mine, labels_ref.at[s], m_send, m_recv, d, {"seq": lax.rem(s + d, 16)})
        )
    for one in small:
        one.start()
    w_ring[2].start()
    w_ring[3].start()
    inputs = embedded(patches_ref, mask_ref, embed_ref)
    tok[a] = layer_norm(inputs, gain_ref[...].astype(F32).reshape(1, D)).astype(BF16)
    for k in range(4):
        t_ring[k].start()
    wts[b] = weight_ref[...]
    for one in small:
        one.wait_recv()

    feature = iota((HD, 1), 0)
    quarter = HD // 4
    place = lax.rem(feature, quarter).astype(F32)
    frequency = jnp.exp(place * (-9.210340371976184 / quarter))
    is_row = feature < 2 * quarter
    is_first = lax.rem(feature, 2 * quarter) < quarter

    def table(pair):
        left = labels_ref[(2 * pair) * step_a + b * step_b].astype(F32)
        right = labels_ref[(2 * pair + 1) * step_a + b * step_b].astype(F32)
        both = side_by_side(left, right)
        angle = jnp.where(is_row, both[1:2], both[2:3]) * frequency
        sine = jnp.sin(angle)
        return jnp.cos(angle), jnp.where(is_first, -sine, 0.0), jnp.where(is_first, 0.0, sine)

    pairs = (a // 2, 1 - a // 2)
    tables = [table(pair) for pair in pairs]

    t_ring[0].wait_recv()
    t_ring[4].start()
    t_ring[1].wait_recv()
    t_ring[5].start()
    w_ring[0].wait_recv()
    w_ring[4].start()
    w_ring[1].wait_recv()
    w_ring[5].start()
    t_ring[2].wait_recv()
    t_ring[3].wait_recv()

    def turn(part, k):
        cosine, ahead, behind = tables[k]
        return (
            part * cosine
            + pltpu.roll(part, HD - quarter, 0) * ahead
            + pltpu.roll(part, quarter, 0) * behind
        )

    def block(k, head):
        tokens = tok[pl.ds(2 * pairs[k], 2)].reshape(2 * ROWS, D)
        projected = lax.dot_general(wts[head], tokens, NT, preferred_element_type=F32)
        return jnp.concatenate(
            [turn(projected[:HD], k), turn(projected[HD : 2 * HD], k), projected[2 * HD :]],
            axis=0,
        ).astype(BF16)

    sends = []

    def send_to(k, off):
        n = len(sends)
        prod[n] = block(k, lax.rem(b + off, 4))
        sends.append(remote(prod.at[n], out_ref.at[b, pairs[k]], p_send, p_recv, n, on_b(off)))
        sends[n].start()

    out_ref[b, pairs[0]] = block(0, b)
    w_ring[2].wait_recv()
    w_ring[3].wait_recv()
    send_to(0, 1)
    send_to(0, 3)
    t_ring[4].wait_recv()
    t_ring[5].wait_recv()
    send_to(1, 1)
    send_to(1, 3)
    w_ring[4].wait_recv()
    w_ring[5].wait_recv()
    send_to(0, 2)
    send_to(1, 2)
    out_ref[b, pairs[1]] = block(1, b)
    for one in sends:
        one.wait_recv()
    for one in w_ring + t_ring + small + sends:
        one.wait_send()


def attention_kernel(n_pack, qkv_ref, labels_ref, owner_ref, out_ref, table_ref, kvs, segs, keys, marks, values):
    core = lax.rem(lax.axis_index("pack"), 2)
    half = ROWS
    wide = 2 * ROWS

    @pl.when(core == 0)
    def _():
        for m in range(8):
            kvs[m] = qkv_ref[m // 2, m % 2]

    @pl.when(core == 1)
    def _():
        lane = iota((3 * HD, wide), 1)
        for m in range(8):
            second, j = (m // 2) % 2, m // 4
            left = qkv_ref[2 * (m % 2), j].astype(F32)
            right = qkv_ref[2 * (m % 2) + 1, j].astype(F32)
            if second:
                left = pltpu.roll(left, half, 1)
            else:
                right = pltpu.roll(right, half, 1)
            kvs[m] = jnp.where(lane < half, left, right).astype(BF16)

    for m in range(8):
        segs[m] = side_by_side(
            labels_ref[2 * m].astype(F32), labels_ref[2 * m + 1].astype(F32)
        )
        fill = jnp.zeros((128 - HD, wide), F32)
        both = kvs[m].astype(F32)
        keys[m] = jnp.concatenate([both[HD : 2 * HD], fill], axis=0).T.astype(BF16)
        values[m] = jnp.concatenate([both[2 * HD :], fill], axis=0).astype(BF16)
        marks[m] = column_of(segs[m][0:1])

    every = jnp.concatenate([labels_ref[k][0:1] for k in range(16)], axis=0)
    total = 16 * ROWS
    starts = [jnp.int32(0)]
    for image in range(1, 8):
        starts.append(jnp.sum((every < image).astype(jnp.int32)))
    starts.append(jnp.int32(total))
    lane = iota((1, 128), 1)
    first = jnp.zeros((1, 128), jnp.int32)
    length = jnp.zeros((1, 128), jnp.int32)
    for image in range(8):
        mine = lane == owner_ref[0, image]
        first = jnp.where(mine, starts[image] // 4, first)
        length = jnp.where(mine, (starts[image + 1] - starts[image]) // 4, length)
    table_ref[0:1, :] = first
    table_ref[1:2, :] = length
    table_ref[2:8, :] = jnp.zeros((6, 128), jnp.int32)

    scale = HD ** (-0.5) * 1.4426950408889634
    low = -0.7 * 3.4028235e38

    size = 2 * wide

    def one_block(g, carry):
        begin = jnp.int32(0)
        end = jnp.int32(total)
        for image in range(1, 8):
            begin = jnp.where(starts[image] <= g * size, starts[image], begin)
        for image in range(7, 0, -1):
            end = jnp.where(starts[image] >= (g + 1) * size, starts[image], end)
        queries = jnp.concatenate(
            [kvs[2 * g, pl.ds(0, HD)], kvs[2 * g + 1, pl.ds(0, HD)]], axis=1
        )
        own = jnp.concatenate([segs[2 * g][0:1], segs[2 * g + 1][0:1]], axis=1)

        def one_step(m, state):
            top, denominator, acc = state
            scores = jnp.dot(keys[m][:, :HD], queries, preferred_element_type=F32)
            scores = jnp.where(marks[m] == own, scores, low)
            new_top = jnp.maximum(top, jnp.max(scores, axis=0, keepdims=True))
            shrink = jnp.exp2((top - new_top) * scale)
            weights = jnp.exp2((scores - new_top) * scale)
            denominator = denominator * shrink + jnp.sum(weights, axis=0, keepdims=True)
            acc = acc * shrink + jnp.dot(
                values[m], weights.astype(BF16), preferred_element_type=F32
            )
            return new_top, denominator, acc

        state = (
            jnp.full((1, size), low, F32),
            jnp.zeros((1, size), F32),
            jnp.zeros((128, size), F32),
        )
        _, denominator, acc = lax.fori_loop(
            begin // wide, (end + wide - 1) // wide, one_step, state
        )
        result = (acc / denominator).T
        for n in range(4):
            out_ref[4 * g + n] = result[n * ROWS : (n + 1) * ROWS].astype(BF16)
        return carry

    lax.fori_loop(0, total // size, one_block, 0)


def merge_kernel(
    n_pack,
    att_ref,
    patches_ref,
    mask_ref,
    embed_ref,
    wo_ref,
    gain_ref,
    wm_ref,
    bias_ref,
    table_ref,
    rows_ref,
    tables_ref,
    heads,
    acc,
    tiles,
    mg,
    wv,
    l_sem,
    h_send,
    h_recv,
    g_send,
    g_recv,
    b_send,
    b_recv,
    z_send,
    z_recv,
    c_send,
    c_recv,
):
    s = lax.axis_index("seq")
    p = lax.axis_index("pack")
    nz = n_pack // 2
    y, x = s // 4, lax.rem(s, 4)

    barrier = pltpu.get_barrier_semaphore()
    for d in range(1, 16):
        pl.semaphore_signal(
            barrier, inc=1, device_id={"seq": lax.rem(s + d, 16)}, device_id_type=MESH
        )
    for d in range(1, n_pack):
        pl.semaphore_signal(
            barrier, inc=1, device_id={"pack": lax.rem(p + d, n_pack)}, device_id_type=MESH
        )
    load = pltpu.make_async_copy(wm_ref, wv, l_sem)
    load.start()
    tables_ref[p] = table_ref[...]
    rows_ref[p, :, :, OUTC:] = jnp.zeros((16, GROUPS, 256 - OUTC), BF16)
    pl.semaphore_wait(barrier, 15 + n_pack - 1)

    out = []
    back = []
    for d in range(1, 16):
        to = lax.rem(s + d, 16)
        back.append(remote(att_ref.at[to], heads.at[s], h_send, h_recv, d, {"seq": to}))
        back[-1].start()
    tabs = []
    for d in range(1, n_pack):
        tabs.append(
            remote(table_ref, tables_ref.at[p], b_send, b_recv, d, {"pack": lax.rem(p + d, n_pack)})
        )
        tabs[-1].start()
    out += back + tabs
    inputs = embedded(patches_ref, mask_ref, embed_ref)
    acc[...] = inputs + jnp.dot(
        att_ref[s][:, :HD], wo_ref[s], preferred_element_type=F32
    )
    for d in range(1, 16):
        back[d - 1].wait_recv()
        head = lax.rem(s + 16 - d, 16)
        acc[...] += jnp.dot(heads[head][:, :HD], wo_ref[head], preferred_element_type=F32)
    normed = layer_norm(acc[...], gain_ref[...].astype(F32).reshape(1, D))
    for t in range(D // 128):
        tiles[t] = normed[:, 128 * t : 128 * (t + 1)]
    for t in range(D // 128):
        for j in range(4):
            mg[s, j, :, 128 * t : 128 * (t + 1)] = tiles[t, pl.ds(j, GROUPS, stride=4), :].astype(
                BF16
            )

    order = {0: 0, -1: 1, 1: 2, 2: 3}

    def device(half, df, dg):
        dx, dy = (df, dg) if half == 0 else (dg, df)
        return lax.rem(y + dy + 4, 4) * 4 + lax.rem(x + dx + 4, 4)

    started = {}

    def send(half, phase, df, dg, kind):
        k = ((half * 2 + phase) * 4 + (order[df] if phase else 0)) * 4 + kind
        blk = device(half, df, dg)
        step = 1 if kind in (0, 2) else -1
        to = device(half, 0, step) if phase else device(half, step, 0)
        if kind < 2:
            ref = mg.at[blk, pl.ds(2 * half, 2)]
        else:
            ref = mg.at[blk, pl.ds(2 * half + kind - 2, 1)]
        one = remote(ref, ref, g_send, g_recv, k, {"seq": to})
        one.start()
        started[half, phase, order[df] if phase else 0, kind] = one
        out.append(one)

    def arrive(half, df, dg):
        phase = 0 if dg == 0 else 1
        off = df if phase == 0 else dg
        k = order[df] if phase else 0
        if off == 2:
            started[half, phase, k, 2].wait_recv()
            started[half, phase, k, 3].wait_recv()
        elif off == -1:
            started[half, phase, k, 0].wait_recv()
            send(half, phase, df, dg, 2)
        else:
            started[half, phase, k, 1].wait_recv()
            send(half, phase, df, dg, 3)
        if phase == 0:
            send(half, 1, df, 0, 0)
            send(half, 1, df, 0, 1)

    done = set()

    def need(half, df, dg):
        if (half, df, dg) not in done and (df, dg) != (0, 0):
            done.add((half, df, dg))
            arrive(half, df, dg)

    z_rings = []

    def launch(first, count, kind):
        one = kind(
            n_pack,
            lambda pack: rows_ref.at[pack, pl.ds(first, count)],
            limits_of(nz, len(z_rings)),
            (z_send, z_recv, c_send, c_recv),
            len(z_rings),
        )
        one.start()
        z_rings.append(one)

    def chunk(first, count, pieces, kind=PackRing):
        blocks = ORDER[first : first + count]
        total = jnp.broadcast_to(
            bias_ref[...].astype(F32).reshape(1, OUTC), (count * GROUPS, OUTC)
        )
        for dx, dy in blocks:
            need(0, dx, dy)
            need(1, dy, dx)
        for j in range(4):
            part = jnp.concatenate([mg[device(0, dx, dy), j] for dx, dy in blocks], axis=0)
            total += lax.dot_general(
                part, wv[:, pl.ds(j * D, D)], NT, preferred_element_type=F32
            )
        total = total.astype(BF16)
        for n in range(count):
            rows_ref[p, first + n, :, :OUTC] = total[n * GROUPS : (n + 1) * GROUPS]
        for n in pieces:
            launch(first, n, kind)
            first += n

    def hop(*which):
        for c, h in which:
            if h <= nz // 2:
                z_rings[c].hop(h)

    for half in range(2):
        send(half, 0, 0, 0, 0)
        send(half, 0, 0, 0, 1)
    for half in range(2):
        send(half, 1, 0, 0, 0)
        send(half, 1, 0, 0, 1)
    for half in range(2):
        need(half, -1, 0)
        need(half, 1, 0)
    for half in range(2):
        need(half, 0, -1)
        need(half, 0, 1)
    load.wait()
    chunk(0, 5, (5,), PackDirect)
    for half in range(2):
        need(half, 2, 0)
    chunk(5, 2, (2,), PackDirect)
    for df in (-1, 1):
        for half in range(2):
            need(half, df, -1)
            need(half, df, 1)
    chunk(7, 4, (4,))
    for half in range(2):
        need(half, 2, -1)
        need(half, 2, 1)
    chunk(11, 5, (3, 2))
    hop((2, 1), (3, 1), (4, 1))
    z_rings[0].share()
    z_rings[1].share()
    for h in range(2, nz // 2 + 1):
        hop((2, h), (3, h), (4, h))
    for one in z_rings:
        one.finish()
        one.drain()
    for one in tabs:
        one.wait_recv()
    for one in out:
        one.wait_send()


def select_kernel(n_pack, arrived_ref, tables_ref, out_ref, rows, sems):
    p = lax.axis_index("pack")
    s = lax.axis_index("seq")
    y, x = s // 4, lax.rem(s, 4)
    loads = []
    for n, (dx, dy) in enumerate(ORDER):
        place = lax.rem(y + dy + 4, 4) * 4 + lax.rem(x + dx + 4, 4)
        start = pl.multiple_of(place * GROUPS, GROUPS)
        loads.append(
            pltpu.make_async_copy(
                arrived_ref.at[:, n], rows.at[:, pl.ds(start, GROUPS)], sems.at[n]
            )
        )
        loads[-1].start()
    for one in loads:
        one.wait()
    total = 4 * MOST
    window = MOST + 16
    for q in range(n_pack):
        mine = iota((1, 128), 1) == p
        first = jnp.sum(jnp.where(mine, tables_ref[q, 0:1, :], 0))
        length = jnp.sum(jnp.where(mine, tables_ref[q, 1:2, :], 0))
        base = pl.multiple_of(jnp.minimum((first // 16) * 16, total - window), 16)
        slot = iota((MOST, window), 0)
        source = iota((MOST, window), 1)
        pick = ((source == slot + (first - base)) & (slot < length)).astype(BF16)
        out_ref[0, q] = jnp.dot(
            pick, rows[q, pl.ds(base, window)], preferred_element_type=F32
        )[:, :OUTC].astype(BF16)


def local(
    patches,
    patch_mask,
    mask_embed,
    norm_gain,
    qkv_weight,
    segment_ids,
    patch_rows,
    patch_column,
    out_weight,
    merge_gain,
    merge_weight,
    merge_bias,
    image_owner,
):
    n_pack = lax.axis_size("pack")
    nz = n_pack // 2
    dma = pltpu.SemaphoreType.DMA
    shape = jax.ShapeDtypeStruct
    embed = mask_embed
    wm = merge_weight.T
    qkv, labels = pl.pallas_call(
        qkv_kernel,
        out_shape=(
            shape((4, 2, 3 * HD, 2 * ROWS), BF16),
            shape((16, 8, ROWS), jnp.int32),
        ),
        in_specs=[VM] * 8,
        out_specs=(VM, VM),
        scratch_shapes=[
            pltpu.VMEM((4, ROWS, D), BF16),
            pltpu.VMEM((4, 3 * HD, D), BF16),
            pltpu.VMEM((6, 3 * HD, 2 * ROWS), BF16),
            pltpu.VMEM((8, ROWS), jnp.int32),
            dma((6,)),
            dma((6,)),
            dma((6,)),
            dma((6,)),
            dma((6,)),
            dma((6,)),
            dma((16,)),
            dma((16,)),
        ],
        compiler_params=pltpu.CompilerParams(
            collective_id=0, has_side_effects=True, vmem_limit_bytes=60 * 2**20
        ),
        name="qkv",
    )(
        patches,
        patch_mask,
        embed,
        norm_gain,
        qkv_weight.T,
        segment_ids,
        patch_rows,
        patch_column,
    )
    attended, table = pl.pallas_call(
        functools.partial(attention_kernel, n_pack),
        out_shape=(shape((16, ROWS, 128), BF16), shape((8, 128), jnp.int32)),
        in_specs=[VM, VM, SM],
        out_specs=(VM, VM),
        scratch_shapes=[
            pltpu.VMEM((8, 3 * HD, 2 * ROWS), BF16),
            pltpu.VMEM((8, 8, 2 * ROWS), F32),
            pltpu.VMEM((8, 2 * ROWS, 128), BF16),
            pltpu.VMEM((8, 2 * ROWS, 1), F32),
            pltpu.VMEM((8, 128, 2 * ROWS), BF16),
        ],
        compiler_params=pltpu.CompilerParams(vmem_limit_bytes=60 * 2**20),
        name="attention",
    )(qkv, labels, image_owner)
    rows, tables = pl.pallas_call(
        functools.partial(merge_kernel, n_pack),
        out_shape=(
            shape((n_pack, 16, GROUPS, 256), BF16),
            shape((n_pack, 8, 128), jnp.int32),
        ),
        in_specs=[VM] * 6 + [ANY, VM, VM],
        out_specs=(VM, VM),
        scratch_shapes=[
            pltpu.VMEM((16, ROWS, 128), BF16),
            pltpu.VMEM((ROWS, D), F32),
            pltpu.VMEM((D // 128, ROWS, 128), F32),
            pltpu.VMEM((16, 4, GROUPS, D), BF16),
            pltpu.VMEM((OUTC, 4 * D), BF16),
            dma,
            dma((16,)),
            dma((16,)),
            dma((64,)),
            dma((64,)),
            dma((n_pack,)),
            dma((n_pack,)),
            dma((10 * nz,)),
            dma((10 * nz,)),
            dma((5 * nz,)),
            dma((5 * nz,)),
        ],
        compiler_params=pltpu.CompilerParams(
            collective_id=1, has_side_effects=True, vmem_limit_bytes=60 * 2**20
        ),
        name="merge",
    )(
        attended,
        patches,
        patch_mask,
        embed,
        out_weight.reshape(HEADS, HD, D),
        merge_gain,
        wm,
        merge_bias,
        table,
    )
    return pl.pallas_call(
        functools.partial(select_kernel, n_pack),
        out_shape=shape((1, n_pack, MOST, OUTC), BF16),
        in_specs=[ANY, VM],
        out_specs=VM,
        scratch_shapes=[pltpu.VMEM((n_pack, 4 * MOST, 256), BF16), dma((16,))],
        compiler_params=pltpu.CompilerParams(vmem_limit_bytes=60 * 2**20),
        name="select",
    )(rows, tables)


def solution(mesh):
    placed = (
        P("pack", "seq", None),
        P("pack", "seq"),
        P(),
        P(),
        P(None, "seq"),
        P("pack", "seq"),
        P("pack", "seq"),
        P("pack", "seq"),
        P(),
        P(),
        P(None, "seq"),
        P("seq"),
        P("pack", None),
    )
    return jax.shard_map(
        local, mesh=mesh, in_specs=placed, out_specs=P("pack", None, None, "seq"), check_vma=False
    )
```

```python
import functools

import jax
import jax.numpy as jnp
from jax import lax
from jax.experimental import pallas as pl
from jax.experimental.pallas import tpu as pltpu
from jax.sharding import PartitionSpec as P

D = 1408
HEADS = 16
HD = 88
ROWS = 192
GROUPS = 48
OUTC = 224
MOST = 192
EPSILON = 1e-06
F32 = jnp.float32
BF16 = jnp.bfloat16
MESH = pl.DeviceIdType.MESH
NT = (((1,), (1,)), ((), ()))
VM = pl.BlockSpec(memory_space=pltpu.VMEM)
ANY = pl.BlockSpec(memory_space=pl.ANY)
SM = pl.BlockSpec(memory_space=pltpu.SMEM)


def iota(shape, axis):
    return lax.broadcasted_iota(jnp.int32, shape, axis)


def column_of(row):
    n = row.shape[1]
    eye = (iota((n, n), 0) == iota((n, n), 1)).astype(BF16)
    wide = jnp.broadcast_to(row, (8, n)).astype(BF16)
    return lax.dot_general(eye, wide, NT, preferred_element_type=F32)[:, :1]


def side_by_side(left, right):
    n = left.shape[1]
    first = (iota((n, 2 * n), 0) == iota((n, 2 * n), 1)).astype(BF16)
    second = (iota((n, 2 * n), 0) + n == iota((n, 2 * n), 1)).astype(BF16)
    return jnp.dot(left.astype(BF16), first, preferred_element_type=F32) + jnp.dot(
        right.astype(BF16), second, preferred_element_type=F32
    )


def layer_norm(values, gain):
    center = values - jnp.mean(values, axis=-1, keepdims=True)
    spread = jnp.mean(center * center, axis=-1, keepdims=True)
    return center * lax.rsqrt(spread + EPSILON) * gain


def embedded(patches_ref, mask_ref, embed_ref):
    chosen = column_of(mask_ref[...].astype(F32))
    return jnp.where(
        chosen > 0.5, embed_ref[...].astype(F32).reshape(1, D), patches_ref[0].astype(F32)
    )

def remote(src, dst, send, recv, k, where):
    return pltpu.make_async_remote_copy(
        src_ref=src,
        dst_ref=dst,
        send_sem=send.at[k],
        recv_sem=recv.at[k],
        device_id=where,
        device_id_type=MESH,
    )


def ring_of_four(own, ref_of, pos, parts, send, recv, to):
    first, second = parts
    before, after = lax.rem(pos + 3, 4), lax.rem(pos + 1, 4)

    def fresh(part, k, where):
        return remote(own(part), ref_of(pos, part), send, recv, k, where)

    def again(slot, part, k, where):
        ref = ref_of(slot, part)
        return remote(ref, ref, send, recv, k, where)

    return [
        fresh(first, 0, to(1)),
        fresh(second, 1, to(3)),
        fresh(second, 2, to(1)),
        fresh(first, 3, to(3)),
        again(before, first, 4, to(1)),
        again(after, second, 5, to(3)),
    ]


class PackRing:
    def __init__(self, n_pack, ref_of, limits, sems, base, own=None):
        self.p = lax.axis_index("pack")
        self.nz = n_pack // 2
        self.z, self.core = self.p // 2, lax.rem(self.p, 2)
        self.ref_of, self.limits, self.sems, self.base, self.own = ref_of, limits, sems, base, own
        self.made = {}

    def go(self, pack, step, k, own=False):
        z_send, z_recv, c_send, c_recv = self.sems
        ref = self.ref_of(pack)
        src = self.own if own and self.own is not None else ref
        if step == 2:
            to = self.z * 2 + 1 - self.core
            one = remote(src, ref, c_send, c_recv, self.base * self.nz + k, {"pack": to})
        else:
            to = lax.rem(self.z + step + self.nz, self.nz) * 2 + self.core
            n = (self.base * 2 + (step + 1) // 2) * self.nz + k
            one = remote(src, ref, z_send, z_recv, n, {"pack": to})
        one.start()
        self.made[step, k] = one

    def start(self):
        for step in (1, -1, 2):
            self.go(self.p, step, 0, own=True)

    def hop(self, h):
        for step, limit in ((1, self.limits[0]), (-1, self.limits[1])):
            if h > limit:
                continue
            self.made[step, h - 1].wait_recv()
            pack = lax.rem(self.z - step * h + self.nz, self.nz) * 2 + self.core
            if h < limit:
                self.go(pack, step, h)
            self.go(pack, 2, h if step == 1 else self.limits[0] + h)

    def finish(self):
        for k in range(self.nz):
            self.made[2, k].wait_recv()

    def drain(self):
        for one in self.made.values():
            one.wait_send()


class PackDirect(PackRing):
    def start(self):
        z_send, z_recv, c_send, c_recv = self.sems
        ref = self.ref_of(self.p)
        self.go(self.p, 2, 0)
        steps = [k for n in range(1, self.nz // 2 + 1) for k in (n, self.nz - n)]
        for k in dict.fromkeys(steps):
            to = lax.rem(self.z + k, self.nz) * 2 + self.core
            one = remote(ref, ref, z_send, z_recv, self.base * 2 * self.nz + k, {"pack": to})
            one.start()
            self.made[1, k] = one

    def share(self):
        for k in range(1, self.nz):
            self.made[1, k].wait_recv()
            self.go(lax.rem(self.z - k + self.nz, self.nz) * 2 + self.core, 2, k)


ORDER = (
    (0, 0), (-1, 0), (1, 0), (0, -1), (0, 1),
    (2, 0), (0, 2),
    (-1, -1), (1, -1), (-1, 1), (1, 1),
    (2, -1), (2, 1), (-1, 2), (1, 2), (2, 2),
)


def limits_of(nz, c):
    low, high = nz - 1 - nz // 2, nz // 2
    return (high, low) if c % 2 == 0 else (low, high)


def qkv_kernel(
    patches_ref,
    mask_ref,
    embed_ref,
    gain_ref,
    weight_ref,
    seg_ref,
    row_ref,
    col_ref,
    out_ref,
    labels_ref,
    tok,
    wts,
    prod,
    mine,
    t_send,
    t_recv,
    w_send,
    w_recv,
    p_send,
    p_recv,
    m_send,
    m_recv,
):
    s = lax.axis_index("seq")
    core = lax.rem(lax.axis_index("pack"), 2)
    y, x = s // 4, lax.rem(s, 4)
    a = x * (1 - core) + y * core
    b = y * (1 - core) + x * core
    step_a, step_b = 1 + 3 * core, 4 - 3 * core

    def on_a(k):
        return {"seq": lax.rem(a + k, 4) * step_a + b * step_b}

    def on_b(k):
        return {"seq": a * step_a + lax.rem(b + k, 4) * step_b}

    barrier = pltpu.get_barrier_semaphore()

    def greet(where):
        pl.semaphore_signal(barrier, inc=1, device_id=where, device_id_type=MESH)

    for d in range(1, 16):
        greet({"seq": lax.rem(s + d, 16)})

    mine[0:1, :] = seg_ref[...]
    mine[1:2, :] = row_ref[...]
    mine[2:3, :] = col_ref[...]
    mine[3:8, :] = jnp.zeros((5, ROWS), jnp.int32)
    labels_ref[s] = mine[...]
    inputs = embedded(patches_ref, mask_ref, embed_ref)
    tok[a] = layer_norm(inputs, gain_ref[...].astype(F32).reshape(1, D)).astype(BF16)
    pl.semaphore_wait(barrier, 15)

    w_ring = ring_of_four(
        lambda part: weight_ref.at[part],
        lambda slot, part: wts.at[slot, part],
        b,
        (pl.ds(0, 136), pl.ds(136, 128)),
        w_send,
        w_recv,
        on_b,
    )
    t_ring = ring_of_four(
        lambda part: tok.at[a, part],
        lambda slot, part: tok.at[slot, part],
        a,
        (pl.ds(0, 96), pl.ds(96, 96)),
        t_send,
        t_recv,
        on_a,
    )
    w_ring[0].start()
    w_ring[1].start()
    small = []
    for d in range(1, 16):
        small.append(
            remote(mine, labels_ref.at[s], m_send, m_recv, d, {"seq": lax.rem(s + d, 16)})
        )
    for one in small:
        one.start()
    w_ring[2].start()
    w_ring[3].start()
    for k in range(4):
        t_ring[k].start()
    wts[b] = weight_ref[...]
    for one in small:
        one.wait_recv()

    feature = iota((HD, 1), 0)
    quarter = HD // 4
    place = lax.rem(feature, quarter).astype(F32)
    frequency = jnp.exp(place * (-9.210340371976184 / quarter))
    is_row = feature < 2 * quarter
    is_first = lax.rem(feature, 2 * quarter) < quarter

    def table(pair):
        left = labels_ref[(2 * pair) * step_a + b * step_b].astype(F32)
        right = labels_ref[(2 * pair + 1) * step_a + b * step_b].astype(F32)
        both = side_by_side(left, right)
        angle = jnp.where(is_row, both[1:2], both[2:3]) * frequency
        sine = jnp.sin(angle)
        return jnp.cos(angle), jnp.where(is_first, -sine, 0.0), jnp.where(is_first, 0.0, sine)

    pairs = (a // 2, 1 - a // 2)
    tables = [table(pair) for pair in pairs]

    t_ring[0].wait_recv()
    t_ring[4].start()
    t_ring[1].wait_recv()
    t_ring[5].start()
    w_ring[0].wait_recv()
    w_ring[4].start()
    w_ring[1].wait_recv()
    w_ring[5].start()
    t_ring[2].wait_recv()
    t_ring[3].wait_recv()

    def turn(part, k):
        cosine, ahead, behind = tables[k]
        return (
            part * cosine
            + pltpu.roll(part, HD - quarter, 0) * ahead
            + pltpu.roll(part, quarter, 0) * behind
        )

    def block(k, head):
        tokens = tok[pl.ds(2 * pairs[k], 2)].reshape(2 * ROWS, D)
        projected = lax.dot_general(wts[head], tokens, NT, preferred_element_type=F32)
        return jnp.concatenate(
            [turn(projected[:HD], k), turn(projected[HD : 2 * HD], k), projected[2 * HD :]],
            axis=0,
        ).astype(BF16)

    sends = []

    def send_to(k, off):
        n = len(sends)
        prod[n] = block(k, lax.rem(b + off, 4))
        sends.append(remote(prod.at[n], out_ref.at[b, pairs[k]], p_send, p_recv, n, on_b(off)))
        sends[n].start()

    out_ref[b, pairs[0]] = block(0, b)
    w_ring[2].wait_recv()
    w_ring[3].wait_recv()
    send_to(0, 1)
    send_to(0, 3)
    t_ring[4].wait_recv()
    t_ring[5].wait_recv()
    send_to(1, 1)
    send_to(1, 3)
    w_ring[4].wait_recv()
    w_ring[5].wait_recv()
    send_to(0, 2)
    send_to(1, 2)
    out_ref[b, pairs[1]] = block(1, b)
    for one in sends:
        one.wait_recv()
    for one in w_ring + t_ring + small + sends:
        one.wait_send()


def attention_kernel(n_pack, qkv_ref, labels_ref, owner_ref, out_ref, table_ref, kvs, segs, keys, marks, values):
    core = lax.rem(lax.axis_index("pack"), 2)
    half = ROWS
    wide = 2 * ROWS

    @pl.when(core == 0)
    def _():
        for m in range(8):
            kvs[m] = qkv_ref[m // 2, m % 2]

    @pl.when(core == 1)
    def _():
        lane = iota((3 * HD, wide), 1)
        for m in range(8):
            second, j = (m // 2) % 2, m // 4
            left = qkv_ref[2 * (m % 2), j].astype(F32)
            right = qkv_ref[2 * (m % 2) + 1, j].astype(F32)
            if second:
                left = pltpu.roll(left, half, 1)
            else:
                right = pltpu.roll(right, half, 1)
            kvs[m] = jnp.where(lane < half, left, right).astype(BF16)

    for m in range(8):
        segs[m] = side_by_side(
            labels_ref[2 * m].astype(F32), labels_ref[2 * m + 1].astype(F32)
        )
        fill = jnp.zeros((128 - HD, wide), F32)
        both = kvs[m].astype(F32)
        keys[m] = jnp.concatenate([both[HD : 2 * HD], fill], axis=0).T.astype(BF16)
        values[m] = jnp.concatenate([both[2 * HD :], fill], axis=0).astype(BF16)
        marks[m] = column_of(segs[m][0:1])

    every = jnp.concatenate([labels_ref[k][0:1] for k in range(16)], axis=0)
    total = 16 * ROWS
    starts = [jnp.int32(0)]
    for image in range(1, 8):
        starts.append(jnp.sum((every < image).astype(jnp.int32)))
    starts.append(jnp.int32(total))
    lane = iota((1, 128), 1)
    first = jnp.zeros((1, 128), jnp.int32)
    length = jnp.zeros((1, 128), jnp.int32)
    for image in range(8):
        mine = lane == owner_ref[0, image]
        first = jnp.where(mine, starts[image] // 4, first)
        length = jnp.where(mine, (starts[image + 1] - starts[image]) // 4, length)
    table_ref[0:1, :] = first
    table_ref[1:2, :] = length
    table_ref[2:8, :] = jnp.zeros((6, 128), jnp.int32)

    scale = HD ** (-0.5) * 1.4426950408889634
    low = -0.7 * 3.4028235e38

    size = 2 * wide

    def one_block(g, carry):
        begin = jnp.int32(0)
        end = jnp.int32(total)
        for image in range(1, 8):
            begin = jnp.where(starts[image] <= g * size, starts[image], begin)
        for image in range(7, 0, -1):
            end = jnp.where(starts[image] >= (g + 1) * size, starts[image], end)
        queries = jnp.concatenate(
            [kvs[2 * g, pl.ds(0, HD)], kvs[2 * g + 1, pl.ds(0, HD)]], axis=1
        )
        own = jnp.concatenate([segs[2 * g][0:1], segs[2 * g + 1][0:1]], axis=1)

        def one_step(m, state):
            top, denominator, acc = state
            scores = jnp.dot(keys[m][:, :HD], queries, preferred_element_type=F32)
            scores = jnp.where(marks[m] == own, scores, low)
            new_top = jnp.maximum(top, jnp.max(scores, axis=0, keepdims=True))
            shrink = jnp.exp2((top - new_top) * scale)
            weights = jnp.exp2((scores - new_top) * scale)
            denominator = denominator * shrink + jnp.sum(weights, axis=0, keepdims=True)
            acc = acc * shrink + jnp.dot(
                values[m], weights.astype(BF16), preferred_element_type=F32
            )
            return new_top, denominator, acc

        state = (
            jnp.full((1, size), low, F32),
            jnp.zeros((1, size), F32),
            jnp.zeros((128, size), F32),
        )
        _, denominator, acc = lax.fori_loop(
            begin // wide, (end + wide - 1) // wide, one_step, state
        )
        result = (acc / denominator).T
        for n in range(4):
            out_ref[4 * g + n] = result[n * ROWS : (n + 1) * ROWS].astype(BF16)
        return carry

    lax.fori_loop(0, total // size, one_block, 0)


def merge_kernel(
    n_pack,
    att_ref,
    patches_ref,
    mask_ref,
    embed_ref,
    wo_hbm,
    gain_ref,
    wm_ref,
    bias_ref,
    table_ref,
    rows_ref,
    tables_ref,
    heads,
    acc,
    tiles,
    mg,
    wv,
    wo_ref,
    l_sem,
    h_send,
    h_recv,
    g_send,
    g_recv,
    b_send,
    b_recv,
    z_send,
    z_recv,
    c_send,
    c_recv,
):
    s = lax.axis_index("seq")
    p = lax.axis_index("pack")
    nz = n_pack // 2
    y, x = s // 4, lax.rem(s, 4)

    barrier = pltpu.get_barrier_semaphore()
    for d in range(1, 16):
        pl.semaphore_signal(
            barrier, inc=1, device_id={"seq": lax.rem(s + d, 16)}, device_id_type=MESH
        )
    for d in range(1, n_pack):
        pl.semaphore_signal(
            barrier, inc=1, device_id={"pack": lax.rem(p + d, n_pack)}, device_id_type=MESH
        )
    first_load = pltpu.make_async_copy(wo_hbm, wo_ref, l_sem.at[0])
    first_load.start()
    load = pltpu.make_async_copy(wm_ref, wv, l_sem.at[1])
    load.start()
    tables_ref[p] = table_ref[...]
    rows_ref[p, :, :, OUTC:] = jnp.zeros((16, GROUPS, 256 - OUTC), BF16)
    pl.semaphore_wait(barrier, 15 + n_pack - 1)

    out = []
    back = []
    for d in range(1, 16):
        to = lax.rem(s + d, 16)
        back.append(remote(att_ref.at[to], heads.at[s], h_send, h_recv, d, {"seq": to}))
        back[-1].start()
    tabs = []
    for d in range(1, n_pack):
        tabs.append(
            remote(table_ref, tables_ref.at[p], b_send, b_recv, d, {"pack": lax.rem(p + d, n_pack)})
        )
        tabs[-1].start()
    out += back + tabs
    inputs = embedded(patches_ref, mask_ref, embed_ref)
    first_load.wait()
    acc[...] = inputs + jnp.dot(
        att_ref[s][:, :HD], wo_ref[s], preferred_element_type=F32
    )
    for d in range(1, 16):
        back[d - 1].wait_recv()
        head = lax.rem(s + 16 - d, 16)
        acc[...] += jnp.dot(heads[head][:, :HD], wo_ref[head], preferred_element_type=F32)
    normed = layer_norm(acc[...], gain_ref[...].astype(F32).reshape(1, D))
    for t in range(D // 128):
        tiles[t] = normed[:, 128 * t : 128 * (t + 1)]
    for t in range(D // 128):
        for j in range(4):
            mg[s, j, :, 128 * t : 128 * (t + 1)] = tiles[t, pl.ds(j, GROUPS, stride=4), :].astype(
                BF16
            )

    order = {0: 0, -1: 1, 1: 2, 2: 3}

    def device(half, df, dg):
        dx, dy = (df, dg) if half == 0 else (dg, df)
        return lax.rem(y + dy + 4, 4) * 4 + lax.rem(x + dx + 4, 4)

    started = {}

    def send(half, phase, df, dg, kind):
        k = ((half * 2 + phase) * 4 + (order[df] if phase else 0)) * 4 + kind
        blk = device(half, df, dg)
        step = 1 if kind in (0, 2) else -1
        to = device(half, 0, step) if phase else device(half, step, 0)
        if kind < 2:
            ref = mg.at[blk, pl.ds(2 * half, 2)]
        else:
            ref = mg.at[blk, pl.ds(2 * half + kind - 2, 1)]
        one = remote(ref, ref, g_send, g_recv, k, {"seq": to})
        one.start()
        started[half, phase, order[df] if phase else 0, kind] = one
        out.append(one)

    def arrive(half, df, dg):
        phase = 0 if dg == 0 else 1
        off = df if phase == 0 else dg
        k = order[df] if phase else 0
        if off == 2:
            started[half, phase, k, 2].wait_recv()
            started[half, phase, k, 3].wait_recv()
        elif off == -1:
            started[half, phase, k, 0].wait_recv()
            send(half, phase, df, dg, 2)
        else:
            started[half, phase, k, 1].wait_recv()
            send(half, phase, df, dg, 3)
        if phase == 0:
            send(half, 1, df, 0, 0)
            send(half, 1, df, 0, 1)

    done = set()

    def need(half, df, dg):
        if (half, df, dg) not in done and (df, dg) != (0, 0):
            done.add((half, df, dg))
            arrive(half, df, dg)

    z_rings = []

    def launch(first, count, kind):
        one = kind(
            n_pack,
            lambda pack: rows_ref.at[pack, pl.ds(first, count)],
            limits_of(nz, len(z_rings)),
            (z_send, z_recv, c_send, c_recv),
            len(z_rings),
        )
        one.start()
        z_rings.append(one)

    def chunk(first, count, pieces, kind=PackRing):
        blocks = ORDER[first : first + count]
        total = jnp.broadcast_to(
            bias_ref[...].astype(F32).reshape(1, OUTC), (count * GROUPS, OUTC)
        )
        for dx, dy in blocks:
            need(0, dx, dy)
            need(1, dy, dx)
        for j in range(4):
            part = jnp.concatenate([mg[device(0, dx, dy), j] for dx, dy in blocks], axis=0)
            total += lax.dot_general(
                part, wv[:, pl.ds(j * D, D)], NT, preferred_element_type=F32
            )
        total = total.astype(BF16)
        for n in range(count):
            rows_ref[p, first + n, :, :OUTC] = total[n * GROUPS : (n + 1) * GROUPS]
        for n in pieces:
            launch(first, n, kind)
            first += n

    def hop(*which):
        for c, h in which:
            if h <= nz // 2:
                z_rings[c].hop(h)

    for half in range(2):
        send(half, 0, 0, 0, 0)
        send(half, 0, 0, 0, 1)
    for half in range(2):
        send(half, 1, 0, 0, 0)
        send(half, 1, 0, 0, 1)
    for half in range(2):
        need(half, -1, 0)
        need(half, 1, 0)
    for half in range(2):
        need(half, 0, -1)
        need(half, 0, 1)
    load.wait()
    chunk(0, 5, (5,), PackDirect)
    for half in range(2):
        need(half, 2, 0)
    chunk(5, 2, (2,), PackDirect)
    for df in (-1, 1):
        for half in range(2):
            need(half, df, -1)
            need(half, df, 1)
    chunk(7, 4, (4,))
    for half in range(2):
        need(half, 2, -1)
        need(half, 2, 1)
    chunk(11, 5, (2, 2, 1))
    hop((2, 1), (3, 1), (4, 1), (5, 1))
    z_rings[0].share()
    z_rings[1].share()
    for h in range(2, nz // 2 + 1):
        hop((2, h), (3, h), (4, h), (5, h))
    for one in z_rings:
        one.finish()
        one.drain()
    for one in tabs:
        one.wait_recv()
    for one in out:
        one.wait_send()


def select_kernel(n_pack, arrived_ref, tables_ref, out_ref, rows, sems):
    p = lax.axis_index("pack")
    s = lax.axis_index("seq")
    y, x = s // 4, lax.rem(s, 4)
    part = n_pack // 2
    loads = []
    for h in range(2):
        packs = pl.ds(h * part, part)
        for n, (dx, dy) in enumerate(ORDER):
            place = lax.rem(y + dy + 4, 4) * 4 + lax.rem(x + dx + 4, 4)
            start = pl.multiple_of(place * GROUPS, GROUPS)
            loads.append(
                pltpu.make_async_copy(
                    arrived_ref.at[packs, n],
                    rows.at[packs, pl.ds(start, GROUPS)],
                    sems.at[16 * h + n],
                )
            )
            loads[-1].start()
    total = 4 * MOST
    window = MOST + 16
    for q in range(n_pack):
        if q % part == 0:
            for one in loads[16 * (q // part) :][:16]:
                one.wait()
        mine = iota((1, 128), 1) == p
        first = jnp.sum(jnp.where(mine, tables_ref[q, 0:1, :], 0))
        length = jnp.sum(jnp.where(mine, tables_ref[q, 1:2, :], 0))
        base = pl.multiple_of(jnp.minimum((first // 16) * 16, total - window), 16)
        slot = iota((MOST, window), 0)
        source = iota((MOST, window), 1)
        pick = ((source == slot + (first - base)) & (slot < length)).astype(BF16)
        out_ref[0, q] = jnp.dot(
            pick, rows[q, pl.ds(base, window)], preferred_element_type=F32
        )[:, :OUTC].astype(BF16)


def local(
    patches,
    patch_mask,
    mask_embed,
    norm_gain,
    qkv_weight,
    segment_ids,
    patch_rows,
    patch_column,
    out_weight,
    merge_gain,
    merge_weight,
    merge_bias,
    image_owner,
):
    n_pack = lax.axis_size("pack")
    nz = n_pack // 2
    dma = pltpu.SemaphoreType.DMA
    shape = jax.ShapeDtypeStruct
    embed = mask_embed
    wm = merge_weight.T
    qkv, labels = pl.pallas_call(
        qkv_kernel,
        out_shape=(
            shape((4, 2, 3 * HD, 2 * ROWS), BF16),
            shape((16, 8, ROWS), jnp.int32),
        ),
        in_specs=[VM] * 8,
        out_specs=(VM, VM),
        scratch_shapes=[
            pltpu.VMEM((4, ROWS, D), BF16),
            pltpu.VMEM((4, 3 * HD, D), BF16),
            pltpu.VMEM((6, 3 * HD, 2 * ROWS), BF16),
            pltpu.VMEM((8, ROWS), jnp.int32),
            dma((6,)),
            dma((6,)),
            dma((6,)),
            dma((6,)),
            dma((6,)),
            dma((6,)),
            dma((16,)),
            dma((16,)),
        ],
        compiler_params=pltpu.CompilerParams(
            collective_id=0, has_side_effects=True, vmem_limit_bytes=60 * 2**20
        ),
        name="qkv",
    )(
        patches,
        patch_mask,
        embed,
        norm_gain,
        qkv_weight.T,
        segment_ids,
        patch_rows,
        patch_column,
    )
    attended, table = pl.pallas_call(
        functools.partial(attention_kernel, n_pack),
        out_shape=(shape((16, ROWS, 128), BF16), shape((8, 128), jnp.int32)),
        in_specs=[VM, VM, SM],
        out_specs=(VM, VM),
        scratch_shapes=[
            pltpu.VMEM((8, 3 * HD, 2 * ROWS), BF16),
            pltpu.VMEM((8, 8, 2 * ROWS), F32),
            pltpu.VMEM((8, 2 * ROWS, 128), BF16),
            pltpu.VMEM((8, 2 * ROWS, 1), F32),
            pltpu.VMEM((8, 128, 2 * ROWS), BF16),
        ],
        compiler_params=pltpu.CompilerParams(vmem_limit_bytes=60 * 2**20),
        name="attention",
    )(qkv, labels, image_owner)
    rows, tables = pl.pallas_call(
        functools.partial(merge_kernel, n_pack),
        out_shape=(
            shape((n_pack, 16, GROUPS, 256), BF16),
            shape((n_pack, 8, 128), jnp.int32),
        ),
        in_specs=[VM] * 4 + [ANY, VM, ANY, VM, VM],
        out_specs=(VM, VM),
        scratch_shapes=[
            pltpu.VMEM((16, ROWS, 128), BF16),
            pltpu.VMEM((ROWS, D), F32),
            pltpu.VMEM((D // 128, ROWS, 128), F32),
            pltpu.VMEM((16, 4, GROUPS, D), BF16),
            pltpu.VMEM((OUTC, 4 * D), BF16),
            pltpu.VMEM((HEADS, HD, D), BF16),
            dma((2,)),
            dma((16,)),
            dma((16,)),
            dma((64,)),
            dma((64,)),
            dma((n_pack,)),
            dma((n_pack,)),
            dma((12 * nz,)),
            dma((12 * nz,)),
            dma((6 * nz,)),
            dma((6 * nz,)),
        ],
        compiler_params=pltpu.CompilerParams(
            collective_id=1, has_side_effects=True, vmem_limit_bytes=60 * 2**20
        ),
        name="merge",
    )(
        attended,
        patches,
        patch_mask,
        embed,
        out_weight.reshape(HEADS, HD, D),
        merge_gain,
        wm,
        merge_bias,
        table,
    )
    return pl.pallas_call(
        functools.partial(select_kernel, n_pack),
        out_shape=shape((1, n_pack, MOST, OUTC), BF16),
        in_specs=[ANY, VM],
        out_specs=VM,
        scratch_shapes=[pltpu.VMEM((n_pack, 4 * MOST, 256), BF16), dma((32,))],
        compiler_params=pltpu.CompilerParams(vmem_limit_bytes=60 * 2**20),
        name="select",
    )(rows, tables)


def solution(mesh):
    placed = (
        P("pack", "seq", None),
        P("pack", "seq"),
        P(),
        P(),
        P(None, "seq"),
        P("pack", "seq"),
        P("pack", "seq"),
        P("pack", "seq"),
        P(),
        P(),
        P(None, "seq"),
        P("seq"),
        P("pack", None),
    )
    return jax.shard_map(
        local, mesh=mesh, in_specs=placed, out_specs=P("pack", None, None, "seq"), check_vma=False
    )
```
